32 devices in a mesh: rows: 16 (over z, x, core), inner: 2 (over y).
Axes of the slice: x: 2, y: 2, z: 4, core: 2. Of those that a mesh axis runs over, the one named last changes fastest.
Arguments:
- p_blocks: bfloat16 [48, 16, 128, 128], P('rows', 'inner'), may hold values from -0.5 to 0.5
- col_lists: int32 [48, 16], replicated, may hold values from 0 to 47, as said below
- fill_lists: int32 [48, 16], replicated, may hold values from 0 to 47, as said below
Outputs:
- purified: float32 [48, 16, 128, 128], P('rows', 'inner')
The draws below stay inside these ranges and needn't reach their ends.
Inputs may be any that keep to these rules, and one draw needn't show every extreme that they name: Entry col_lists[i, s] names a block row whose owner (entry // 3) lies within 2 owners of row i's owner (i // 3), counting around the end. Over the 3 block rows of one owner, the slots of one inner group name block rows of any one owner at most 5 times, and some owner exactly 5 times. Entries may repeat within a row. `fill_lists`: the 16 entries of a row are distinct and name block rows whose owners lie within 4 owners of the row's owner, counting around the end.
All inputs are finite; a program needn't handle non-finite values.
Results may differ from the reference program's by a relative error of at most 0.02.
Values may be sent and summed in bfloat16 or wider, within the bound.
No kernel may reach another device: no remote copies, remote signals or barrier semaphores. Data moves between devices by JAX's collectives and lax.ppermute only.
A program may use at most 128 MiB of HBM per device.

```python
import jax
import jax.numpy as jnp
from jax import lax

BS = 128
K_ROW = 16
FILL = 16
REACH = 2
RB_DEV = 3
NB = 48
N_INNER = 2


def draw_col_lists(key, part):
    owner_count = NB // RB_DEV
    owner_span = 2 * REACH + 1
    slot_count = K_ROW // N_INNER
    shift_key, local_key = jax.random.split(key)
    shifts = jax.random.randint(shift_key, (owner_count, N_INNER), 0, owner_span)
    entries = jnp.arange(RB_DEV)[:, None] * slot_count + jnp.arange(slot_count)[None, :]
    distance = (entries[None, None, :, :] + shifts[:, :, None, None]) % owner_span - REACH
    owners = (jnp.arange(owner_count)[:, None, None, None] + distance) % owner_count
    within = jax.random.randint(local_key, (owner_count, N_INNER, RB_DEV, slot_count), 0, RB_DEV)
    target = owners * RB_DEV + within
    return jnp.transpose(target, (0, 2, 1, 3)).reshape(NB, K_ROW).astype(jnp.int32)


def draw_fill_lists(key, part):
    owner_count = NB // RB_DEV
    window = (4 * REACH + 1) * RB_DEV
    row_keys = jax.random.split(jax.random.fold_in(key, 7), NB)
    chosen = jax.vmap(lambda k: jax.random.permutation(k, window)[:FILL])(row_keys)
    row_owner = jnp.arange(NB) // RB_DEV
    owners = (row_owner[:, None] - 2 * REACH + chosen // RB_DEV) % owner_count
    return (owners * RB_DEV + chosen % RB_DEV).astype(jnp.int32)


def shard_levels(stream_key, dims, cuts, least, largest):
    def one(position, parts):
        steps = jax.random.uniform(jax.random.fold_in(jax.random.fold_in(stream_key, 6), position), (parts,), jnp.float32, least / len(cuts), largest / len(cuts))
        return jnp.repeat(jnp.exp(steps), dims[position] // parts).reshape((-1,) + (1,) * (len(dims) - position - 1))

    level = one(*cuts[0])
    for cut in cuts[1:]:
        level = level * one(*cut)
    return level


def normal_values(stream_key, dims, width, bound, cuts=(), kind=jnp.bfloat16):
    values = width * jax.random.normal(stream_key, dims, jnp.float32)
    if cuts:
        values = values * shard_levels(stream_key, dims, cuts, -0.22, 0.18)
    return jnp.clip(values, -bound, bound).astype(kind)


def setup_inputs(seed: int = 0) -> dict:
    streams_of = jax.random.split(jax.random.key(seed), 4)
    return {
        "p_blocks": normal_values(streams_of[0], (NB, K_ROW, BS, BS), (K_ROW * BS // 16) ** -0.5, 0.5, ((0, 16), (1, 2))),
        "col_lists": draw_col_lists(jax.random.fold_in(streams_of[3], 71), 0),
        "fill_lists": draw_fill_lists(jax.random.fold_in(streams_of[3], 71), 0),
    }


def group_sum(left_blocks, right_blocks, remote_lists, fill_row):
    selector = (remote_lists[:, :, None] == fill_row[None, None, :]).astype(jnp.float32)
    products = jnp.einsum("sxy,suyz->suxz", left_blocks.astype(jnp.float32), right_blocks.astype(jnp.float32), precision=lax.Precision.HIGHEST)
    slot_count = K_ROW // N_INNER
    products = products.reshape((N_INNER, slot_count) + products.shape[1:])
    selector = selector.reshape((N_INNER, slot_count) + selector.shape[1:])
    pieces = jnp.einsum("qsuv,qsuxz->qvxz", selector, products, precision=lax.Precision.HIGHEST)
    rounded = lax.optimization_barrier(pieces.astype(jnp.bfloat16))
    return jnp.sum(rounded.astype(jnp.float32), axis=0)


def reference(p_blocks, col_lists, fill_lists):
    row_ids = jnp.arange(p_blocks.shape[0], dtype=jnp.int32)

    def first_row(row_index):
        targets = col_lists[row_index]
        return group_sum(p_blocks[row_index], p_blocks[targets], col_lists[targets], fill_lists[row_index])

    square = lax.map(first_row, row_ids)
    square_low = square.astype(jnp.bfloat16)

    def second_row(row_index):
        targets = col_lists[row_index]
        return group_sum(p_blocks[row_index], square_low[targets], fill_lists[targets], fill_lists[row_index])

    cubed = lax.map(second_row, row_ids)
    return 3.0 * square - 2.0 * cubed
```

```python
import functools

import jax
import jax.numpy as jnp
from jax import lax
from jax.experimental import pallas as pl
from jax.experimental.pallas import tpu as pltpu
from jax.sharding import PartitionSpec as P

REACH = 2
BAND = 2 * REACH + 1
WIDE = 4 * REACH + 1
VMEM = pl.BlockSpec(memory_space=pltpu.VMEM)
SMEM = pl.BlockSpec(memory_space=pltpu.SMEM)
PARAMS = pltpu.CompilerParams(vmem_limit_bytes=56 * 1024 * 1024)


def call(kernel, ins, outs, scratch=()):
    specs = [SMEM if x.dtype == jnp.int32 else VMEM for x in ins]
    many = isinstance(outs, (list, tuple))
    return pl.pallas_call(
        kernel,
        out_shape=tuple(outs) if many else outs,
        in_specs=specs,
        out_specs=tuple(VMEM for _ in outs) if many else VMEM,
        scratch_shapes=list(scratch),
        compiler_params=PARAMS,
    )(*ins)


def offsets(j):
    first = j < 2
    return {
        "own": 0,
        "x": jnp.where(first, 2, -2),
        "core": jnp.where(j % 2 == 0, 1, -1),
        "core_x": jnp.where(first, 1, -1),
        "z": jnp.where(first, -2, 2),
        "core_z": jnp.where(first, -1, 1),
    }


def per_device(p_blocks, col_lists, fill_lists):
    rb, slots, bs, _ = p_blocks.shape
    nb, k_row = col_lists.shape
    fill = fill_lists.shape[1]
    n_rows = lax.axis_size("rows")
    n = lax.axis_size("inner")
    part = bs // n
    width = rb * bs
    bf16, f32 = jnp.bfloat16, jnp.float32
    shape = jax.ShapeDtypeStruct
    half = fill // 2

    def shift(m):
        return [(i, (i + m) % n) for i in range(n)]

    def along(r):
        group, j = divmod(r, 4)
        return (group + (1 if j < 2 else -1)) % (n_rows // 4) * 4 + j

    flip_x = [(r, r ^ 2) for r in range(n_rows)]
    flip_core = [(r, r ^ 1) for r in range(n_rows)]
    move_z = [(r, along(r)) for r in range(n_rows)]
    core_x = [(r, r ^ 1) for r in range(n_rows) if r % 4 in (0, 3)]
    core_z = [(r, r ^ 1) for r in range(n_rows) if r % 4 in (1, 2)]

    def send(x, axis, pairs):
        return lax.ppermute(x, axis, pairs)

    def slice_at(index):
        return pl.ds(pl.multiple_of(index * part, part), part)

    def wrapped(x):
        return jnp.where(x < 0, x + nb, jnp.where(x >= nb, x - nb, x))

    def pack(p_ref, own_ref, rest_ref, turned):
        q = lax.axis_index("inner")
        for i in range(rb):
            for s in range(slots):
                turned[i, s] = p_ref[i, s].T
                own_ref[i, s] = turned[i, s, slice_at(q), :]
                for m in range(1, n):
                    rest_ref[m - 1, i, s] = turned[i, s, slice_at(lax.rem(q + m, n)), :]

    own, rest = call(
        pack,
        [p_blocks],
        [shape((rb, slots, part, bs), bf16), shape((n - 1, rb, slots, part, bs), bf16)],
        [pltpu.VMEM((rb, slots, bs, bs), bf16)],
    )

    def received(parts):
        return parts[0][None] if n == 2 else jnp.stack(parts)

    def nth(x, m):
        return x.reshape(x.shape[1:]) if n == 2 else x[m]

    got = received([send(nth(rest, m - 1), "inner", shift(m)) for m in range(1, n)])
    x_own = send(own, "rows", flip_x)
    x_got = send(got, "rows", flip_x)
    z_own = send(x_own, "rows", move_z)
    z_got = send(x_got, "rows", move_z)
    if n == 2:
        left = send(own, "inner", shift(1))
    else:
        left = lax.all_gather(p_blocks, "inner", axis=0)
    c_own, c_got = send(own, "rows", flip_core), send(got, "rows", flip_core)
    cx_own, cx_got = send(x_own, "rows", core_x), send(x_got, "rows", core_x)
    cz_own, cz_got = send(z_own, "rows", core_z), send(z_got, "rows", core_z)

    def band(col_ref, own_ref, rest_ref, got_ref, left_ref, out_ref):
        o = lax.axis_index("rows")
        q = lax.axis_index("inner")
        out_ref[...] = jnp.zeros(out_ref.shape, bf16)

        def place(row, i, slot, block):
            c = wrapped(col_ref[row, slot] - rb * (o - REACH))
            return pl.multiple_of(c * bs, bs), pl.ds(i * bs, bs), block

        def add(base, lanes, at, value):
            where = pl.ds(pl.multiple_of(base + at * part, part), part)
            out_ref[where, lanes] = (out_ref[where, lanes].astype(f32) + value.astype(f32)).astype(bf16)

        for i in range(rb):
            row = o * rb + i
            for s in range(slots):
                c = wrapped(col_ref[row, q * slots + s] - rb * (o - REACH)) * bs
                lanes = pl.ds(i * bs, bs)
                add(c, lanes, q, own_ref[i, s])
                for m in range(1, n):
                    add(c, lanes, lax.rem(q + m, n), rest_ref[m - 1, i, s])
                for m in range(1, n):
                    g = lax.rem(q - m + n, n)
                    c = wrapped(col_ref[row, g * slots + s] - rb * (o - REACH)) * bs
                    if n == 2:
                        add(c, lanes, q, got_ref[0, i, s])
                        add(c, lanes, g, left_ref[i, s])
                    else:
                        where = pl.ds(pl.multiple_of(c, bs), bs)
                        block = left_ref[g, i, s].T.astype(f32)
                        out_ref[where, lanes] = (out_ref[where, lanes].astype(f32) + block).astype(bf16)

    left_band = call(
        band, [col_lists, own, rest, got, left], shape((BAND * width, width), bf16)
    )

    span = BAND * rb * part
    wide = WIDE * rb * part
    owner_rows = rb * part

    def square_term(col_ref, d, own_ref, got_ref, left_ref, dense, acc_ref, first=False):
        o = lax.axis_index("rows")
        q = lax.axis_index("inner")
        source = lax.rem(o + d + n_rows, n_rows)
        dense[...] = jnp.zeros(dense.shape, bf16)

        def add(k, slot, value):
            c = wrapped(col_ref[source * rb + k, slot] - rb * (source - REACH))
            where, lanes = slice_at(c), pl.ds(k * bs, bs)
            dense[where, lanes] = (dense[where, lanes].astype(f32) + value.astype(f32)).astype(bf16)

        for s in range(slots):
            for k in range(rb):
                add(k, q * slots + s, own_ref[k, s])
                for m in range(1, n):
                    g = lax.rem(q - m + n, n)
                    add(k, g * slots + s, got_ref[m - 1, k, s])
        weights = left_ref[pl.ds(pl.multiple_of((d + REACH) * width, width), width), :]
        term = jnp.dot(dense[...], weights, preferred_element_type=f32)
        where = pl.ds(pl.multiple_of((d + REACH) * owner_rows, owner_rows), span)
        if first:
            acc_ref[...] = jnp.zeros(acc_ref.shape, f32)
            acc_ref[where, :] = term
        else:
            acc_ref[where, :] += term

    def square_near(col, w, wg, c, cg, x, xg, cx, cxg, left_ref, acc_ref, dense):
        j = lax.rem(lax.axis_index("rows"), 4)
        d = offsets(j)
        square_term(col, 0, w, wg, left_ref, dense, acc_ref, first=True)
        square_term(col, d["core"], c, cg, left_ref, dense, acc_ref)
        square_term(col, d["x"], x, xg, left_ref, dense, acc_ref)

        @pl.when((j == 1) | (j == 2))
        def _():
            square_term(col, d["core_x"], cx, cxg, left_ref, dense, acc_ref)

    acc = call(
        square_near,
        [col_lists, own, got, c_own, c_got, x_own, x_got, cx_own, cx_got, left_band],
        shape((wide, width), f32),
        [pltpu.VMEM((span, width), bf16)],
    )

    def kept(fill_ref, i, v):
        o = lax.axis_index("rows")
        return slice_at(wrapped(fill_ref[o * rb + i, v] - rb * (o - 2 * REACH)))

    def square_far(col, fill_ref, acc_in, z, zg, cz, czg, left_ref, sq_ref, low0, low1, acc_ref, dense):
        j = lax.rem(lax.axis_index("rows"), 4)
        d = offsets(j)
        acc_ref[...] = acc_in[...]
        square_term(col, d["z"], z, zg, left_ref, dense, acc_ref)

        @pl.when((j == 0) | (j == 3))
        def _():
            square_term(col, d["core_z"], cz, czg, left_ref, dense, acc_ref)

        for i in range(rb):
            for v in range(fill):
                value = acc_ref[kept(fill_ref, i, v), pl.ds(i * bs, bs)]
                sq_ref[i, v] = value
                (low0 if v < half else low1)[i, v % half] = value.astype(bf16)

    low_shape = shape((rb, half, part, bs), bf16)
    square, low0, low1 = call(
        square_far,
        [col_lists, fill_lists, acc, z_own, z_got, cz_own, cz_got, left_band],
        [shape((rb, fill, part, bs), f32), low_shape, low_shape],
        [pltpu.VMEM((wide, width), f32), pltpu.VMEM((span, width), bf16)],
    )

    x0, x1 = send(low0, "rows", flip_x), send(low1, "rows", flip_x)
    z0, z1 = send(x0, "rows", move_z), send(x1, "rows", move_z)
    c0, c1 = send(low0, "rows", flip_core), send(low1, "rows", flip_core)
    cx0, cx1 = send(x0, "rows", core_x), send(x1, "rows", core_x)
    cz0, cz1 = send(z0, "rows", core_z), send(z1, "rows", core_z)

    def cube_term(fill_ref, d, reach, ref0, ref1, left_ref, dense, acc_ref, first=False):
        o = lax.axis_index("rows")
        source = lax.rem(o + d + n_rows, n_rows)
        blocks = (WIDE - reach) * rb
        start = jnp.maximum(d, 0) * rb
        rows = blocks * part
        dense[:rows, :] = jnp.zeros((rows, width), bf16)
        for v in range(fill):
            for k in range(rb):
                c = wrapped(fill_ref[source * rb + k, v] - rb * (o - 2 * REACH)) - start

                @pl.when((c >= 0) & (c < blocks))
                def _():
                    dense[slice_at(c), pl.ds(k * bs, bs)] = (ref0 if v < half else ref1)[k, v % half]

        weights = left_ref[pl.ds(pl.multiple_of((d + REACH) * width, width), width), :]
        term = jnp.dot(dense[:rows, :], weights, preferred_element_type=f32)
        if first:
            acc_ref[...] = term
        else:
            acc_ref[pl.ds(pl.multiple_of(start * part, rb * part), rows), :] += term

    def cube_near(fill_ref, w0, w1, c0, c1, x0, x1, cx0, cx1, left_ref, acc_ref, dense):
        j = lax.rem(lax.axis_index("rows"), 4)
        d = offsets(j)
        cube_term(fill_ref, 0, 0, w0, w1, left_ref, dense, acc_ref, first=True)
        cube_term(fill_ref, d["core"], 1, c0, c1, left_ref, dense, acc_ref)
        cube_term(fill_ref, d["x"], 2, x0, x1, left_ref, dense, acc_ref)

        @pl.when((j == 1) | (j == 2))
        def _():
            cube_term(fill_ref, d["core_x"], 1, cx0, cx1, left_ref, dense, acc_ref)

    acc = call(
        cube_near,
        [fill_lists, low0, low1, c0, c1, x0, x1, cx0, cx1, left_band],
        shape((wide, width), f32),
        [pltpu.VMEM((wide, width), bf16)],
    )

    def cube_far(fill_ref, acc_in, z0, z1, cz0, cz1, left_ref, sq_ref, keep_ref, give_ref, acc_ref, dense):
        q = lax.axis_index("inner")
        j = lax.rem(lax.axis_index("rows"), 4)
        d = offsets(j)
        acc_ref[...] = acc_in[...]
        cube_term(fill_ref, d["z"], 2, z0, z1, left_ref, dense, acc_ref)

        @pl.when((j == 0) | (j == 3))
        def _():
            cube_term(fill_ref, d["core_z"], 1, cz0, cz1, left_ref, dense, acc_ref)

        def result(i, v):
            return 3.0 * sq_ref[i, v] - 2.0 * acc_ref[kept(fill_ref, i, v), pl.ds(i * bs, bs)]

        for i in range(rb):
            for s in range(slots):
                keep_ref[i, s] = result(i, q * slots + s)
                for m in range(1, n):
                    give_ref[m - 1, i, s] = result(i, lax.rem(q + m, n) * slots + s).astype(bf16)

    keep, give = call(
        cube_far,
        [fill_lists, acc, z0, z1, cz0, cz1, left_band, square],
        [shape((rb, slots, part, bs), f32), shape((n - 1, rb, slots, part, bs), bf16)],
        [pltpu.VMEM((wide, width), f32), pltpu.VMEM((wide, width), bf16)],
    )
    taken = received([send(nth(give, m - 1), "inner", shift(m)) for m in range(1, n)])

    def join(keep_ref, taken_ref, out_ref, turned):
        q = lax.axis_index("inner")
        for i in range(rb):
            for s in range(slots):
                turned[i, s, slice_at(q), :] = keep_ref[i, s]
                for m in range(1, n):
                    turned[i, s, slice_at(lax.rem(q - m + n, n)), :] = taken_ref[m - 1, i, s].astype(f32)
                out_ref[i, s] = turned[i, s].T

    return call(
        join,
        [keep, taken],
        shape((rb, slots, bs, bs), f32),
        [pltpu.VMEM((rb, slots, bs, bs), f32)],
    )


def solution(mesh):
    in_specs = (P("rows", "inner", None, None), P(), P())
    out_specs = P("rows", "inner", None, None)
    return jax.shard_map(
        per_device, mesh=mesh, in_specs=in_specs, out_specs=out_specs, check_vma=False
    )
```

```python
import jax
import jax.numpy as jnp
from jax import lax
from jax.experimental import pallas as pl
from jax.experimental.pallas import tpu as pltpu
from jax.sharding import PartitionSpec as P

REACH = 2
BAND = 2 * REACH + 1
WIDE = 4 * REACH + 1
VMEM = pl.BlockSpec(memory_space=pltpu.VMEM)
SMEM = pl.BlockSpec(memory_space=pltpu.SMEM)
PARAMS = pltpu.CompilerParams(vmem_limit_bytes=16 * 1024 * 1024)


def call(kernel, ins, outs, scratch=(), aliases=None, resident=True):
    specs = [SMEM if x.dtype == jnp.int32 else VMEM for x in ins]
    if resident:
        outs = [pltpu.VMEM(x.shape, x.dtype) for x in outs]
    ins = [
        x if x.dtype == jnp.int32 else pltpu.with_memory_space_constraint(x, pltpu.VMEM)
        for x in ins
    ]
    return pl.pallas_call(
        kernel,
        out_shape=tuple(outs),
        in_specs=specs,
        out_specs=tuple(VMEM for _ in outs),
        scratch_shapes=list(scratch),
        input_output_aliases=aliases or {},
        compiler_params=PARAMS,
    )(*ins)


def after(x, *others):
    return lax.optimization_barrier((x, *others))[0]


def offsets(j):
    first = j < 2
    return {
        "own": 0,
        "x": jnp.where(first, 2, -2),
        "core": jnp.where(j % 2 == 0, 1, -1),
        "core_x": jnp.where(first, 1, -1),
        "z": jnp.where(first, -2, 2),
        "core_z": jnp.where(first, -1, 1),
    }


def per_device(p_blocks, col_lists, fill_lists):
    rb, slots, bs, _ = p_blocks.shape
    nb, k_row = col_lists.shape
    fill = fill_lists.shape[1]
    n_rows = lax.axis_size("rows")
    n = lax.axis_size("inner")
    part = bs // n
    width = rb * bs
    bf16, f32 = jnp.bfloat16, jnp.float32
    shape = jax.ShapeDtypeStruct
    half = fill // 2

    def shift(m):
        return [(i, (i + m) % n) for i in range(n)]

    def along(r):
        group, j = divmod(r, 4)
        return (group + (1 if j < 2 else -1)) % (n_rows // 4) * 4 + j

    flip_x = [(r, r ^ 2) for r in range(n_rows)]
    flip_core = [(r, r ^ 1) for r in range(n_rows)]
    move_z = [(r, along(r)) for r in range(n_rows)]
    core_x = [(r, r ^ 1) for r in range(n_rows) if r % 4 in (0, 3)]
    core_z = [(r, r ^ 1) for r in range(n_rows) if r % 4 in (1, 2)]

    def send(x, axis, pairs):
        return lax.ppermute(x, axis, pairs)

    def slice_at(index):
        return pl.ds(pl.multiple_of(index * part, part), part)

    def wrapped(x):
        return jnp.where(x < 0, x + nb, jnp.where(x >= nb, x - nb, x))

    def pack(p_ref, own_ref, rest_ref, turned):
        q = lax.axis_index("inner")
        for i in range(rb):
            for s in range(slots):
                turned[i, s] = p_ref[i, s].T
                own_ref[i, s] = turned[i, s, slice_at(q), :]
                for m in range(1, n):
                    rest_ref[m - 1, i, s] = turned[i, s, slice_at(lax.rem(q + m, n)), :]

    own, rest = call(
        pack,
        [p_blocks],
        [shape((rb, slots, part, bs), bf16), shape((n - 1, rb, slots, part, bs), bf16)],
        [pltpu.VMEM((rb, slots, bs, bs), bf16)],
    )
    lists = jnp.concatenate([col_lists, fill_lists], axis=0)

    def received(parts):
        return parts[0][None] if n == 2 else jnp.stack(parts)

    def nth(x, m):
        return x.reshape(x.shape[1:]) if n == 2 else x[m]

    def add(ref, where, lanes, value):
        ref[where, lanes] = (ref[where, lanes].astype(f32) + value.astype(f32)).astype(bf16)

    def band_own(lists_ref, own_ref, rest_ref, out_ref):
        o = lax.axis_index("rows")
        q = lax.axis_index("inner")
        out_ref[...] = jnp.zeros(out_ref.shape, bf16)
        for s in range(slots):
            for i in range(rb):
                c = wrapped(lists_ref[o * rb + i, q * slots + s] - rb * (o - REACH)) * n
                lanes = pl.ds(i * bs, bs)
                add(out_ref, slice_at(c + q), lanes, own_ref[i, s])
                for m in range(1, n):
                    add(out_ref, slice_at(c + lax.rem(q + m, n)), lanes, rest_ref[m - 1, i, s])

    def band_other(lists_ref, in_ref, got_ref, left_ref, out_ref):
        o = lax.axis_index("rows")
        q = lax.axis_index("inner")
        for s in range(slots):
            for i in range(rb):
                lanes = pl.ds(i * bs, bs)
                for m in range(1, n):
                    g = lax.rem(q - m + n, n)
                    c = wrapped(lists_ref[o * rb + i, g * slots + s] - rb * (o - REACH))
                    if n == 2:
                        add(out_ref, slice_at(c * n + q), lanes, got_ref[0, i, s])
                        add(out_ref, slice_at(c * n + g), lanes, left_ref[i, s])
                    else:
                        add(out_ref, pl.ds(pl.multiple_of(c * bs, bs), bs), lanes, left_ref[g, i, s].T)

    band_shape = shape((BAND * width, width), bf16)
    (band,) = call(band_own, [lists, own, rest], [band_shape])

    got = received([send(nth(rest, m - 1), "inner", shift(m)) for m in range(1, n)])
    got = after(got, band)
    x_own = send(own, "rows", flip_x)
    x_got = send(got, "rows", flip_x)
    if n == 2:
        left = send(after(own, got), "inner", shift(1))
    else:
        left = lax.all_gather(p_blocks, "inner", axis=0)
    z_own = send(x_own, "rows", move_z)
    z_got = send(x_got, "rows", move_z)
    c_own, c_got = send(own, "rows", flip_core), send(got, "rows", flip_core)
    cx_own, cx_got = send(x_own, "rows", core_x), send(x_got, "rows", core_x)
    cz_own = send(z_own, "rows", core_z)
    (band,) = call(band_other, [lists, band, got, left], [band_shape], aliases={1: 0})

    span = BAND * rb * part
    wide = WIDE * rb * part
    owner_rows = rb * part
    acc_shape = shape((wide, width), f32)

    def square_term(lists_ref, d, own_ref, got_ref, left_ref, dense, acc_ref, first=False):
        o = lax.axis_index("rows")
        q = lax.axis_index("inner")
        source = lax.rem(o + d + n_rows, n_rows)
        dense[...] = jnp.zeros(dense.shape, bf16)

        def place(k, slot, value):
            c = wrapped(lists_ref[source * rb + k, slot] - rb * (source - REACH))
            add(dense, slice_at(c), pl.ds(k * bs, bs), value)

        for s in range(slots):
            for k in range(rb):
                place(k, q * slots + s, own_ref[k, s])
                for m in range(1, n):
                    place(k, lax.rem(q - m + n, n) * slots + s, got_ref[m - 1, k, s])
        weights = left_ref[pl.ds(pl.multiple_of((d + REACH) * width, width), width), :]
        term = jnp.dot(dense[...], weights, preferred_element_type=f32)
        where = pl.ds(pl.multiple_of((d + REACH) * owner_rows, owner_rows), span)
        if first:
            acc_ref[...] = jnp.zeros(acc_ref.shape, f32)
            acc_ref[where, :] = term
        else:
            acc_ref[where, :] += term

    def square_near(col, w, wg, c, cg, x, xg, cx, cxg, left_ref, acc_ref, dense):
        j = lax.rem(lax.axis_index("rows"), 4)
        d = offsets(j)
        square_term(col, 0, w, wg, left_ref, dense, acc_ref, first=True)
        square_term(col, d["core"], c, cg, left_ref, dense, acc_ref)
        square_term(col, d["x"], x, xg, left_ref, dense, acc_ref)

        @pl.when((j == 1) | (j == 2))
        def _():
            square_term(col, d["core_x"], cx, cxg, left_ref, dense, acc_ref)

    (acc,) = call(
        square_near,
        [lists, own, got, c_own, c_got, x_own, x_got, cx_own, cx_got, band],
        [acc_shape],
        [pltpu.VMEM((span, width), bf16)],
    )
    cz_got = send(after(z_got, acc), "rows", core_z)

    def kept(lists_ref, i, v):
        o = lax.axis_index("rows")
        return slice_at(wrapped(lists_ref[nb + o * rb + i, v] - rb * (o - 2 * REACH)))

    def square_far(col, acc_in, z, zg, cz, czg, left_ref, acc_ref, sq_ref, low0, low1, dense):
        j = lax.rem(lax.axis_index("rows"), 4)
        d = offsets(j)
        square_term(col, d["z"], z, zg, left_ref, dense, acc_ref)

        @pl.when((j == 0) | (j == 3))
        def _():
            square_term(col, d["core_z"], cz, czg, left_ref, dense, acc_ref)

        for v in range(fill):
            for i in range(rb):
                value = acc_ref[kept(col, i, v), pl.ds(i * bs, bs)]
                sq_ref[i, v] = value
                (low0 if v < half else low1)[i, v % half] = value.astype(bf16)

    low_shape = shape((rb, half, part, bs), bf16)
    _, square, low0, low1 = call(
        square_far,
        [lists, acc, z_own, z_got, cz_own, cz_got, band],
        [acc_shape, shape((rb, fill, part, bs), f32), low_shape, low_shape],
        [pltpu.VMEM((span, width), bf16)],
        aliases={1: 0},
    )

    def cube_term(lists_ref, d, reach, ref0, ref1, left_ref, dense, acc_ref, first=False):
        o = lax.axis_index("rows")
        source = lax.rem(o + d + n_rows, n_rows)
        blocks = (WIDE - reach) * rb
        start = jnp.maximum(d, 0) * rb
        rows = blocks * part
        dense[:rows, :] = jnp.zeros((rows, width), bf16)
        for v in range(fill):
            for k in range(rb):
                c = wrapped(lists_ref[nb + source * rb + k, v] - rb * (o - 2 * REACH)) - start

                @pl.when((c >= 0) & (c < blocks))
                def _():
                    dense[slice_at(c), pl.ds(k * bs, bs)] = (ref0 if v < half else ref1)[k, v % half]

        weights = left_ref[pl.ds(pl.multiple_of((d + REACH) * width, width), width), :]
        term = jnp.dot(dense[:rows, :], weights, preferred_element_type=f32)
        if first:
            acc_ref[...] = term
        else:
            acc_ref[pl.ds(pl.multiple_of(start * part, rb * part), rows), :] += term

    def cube_own(lists_ref, w0, w1, c0, c1, left_ref, acc_ref, dense):
        d = offsets(lax.rem(lax.axis_index("rows"), 4))
        cube_term(lists_ref, 0, 0, w0, w1, left_ref, dense, acc_ref, first=True)
        cube_term(lists_ref, d["core"], 1, c0, c1, left_ref, dense, acc_ref)

    def cube_near(lists_ref, acc_in, x0, x1, cx0, cx1, left_ref, acc_ref, dense):
        j = lax.rem(lax.axis_index("rows"), 4)
        d = offsets(j)
        cube_term(lists_ref, d["x"], 2, x0, x1, left_ref, dense, acc_ref)

        @pl.when((j == 1) | (j == 2))
        def _():
            cube_term(lists_ref, d["core_x"], 1, cx0, cx1, left_ref, dense, acc_ref)

    def cube_far(lists_ref, acc_in, z0, z1, cz0, cz1, left_ref, sq_ref, acc_ref, keep_ref, give_ref, dense):
        q = lax.axis_index("inner")
        j = lax.rem(lax.axis_index("rows"), 4)
        d = offsets(j)
        cube_term(lists_ref, d["z"], 2, z0, z1, left_ref, dense, acc_ref)

        @pl.when((j == 0) | (j == 3))
        def _():
            cube_term(lists_ref, d["core_z"], 1, cz0, cz1, left_ref, dense, acc_ref)

        def result(i, v):
            return 3.0 * sq_ref[i, v] - 2.0 * acc_ref[kept(lists_ref, i, v), pl.ds(i * bs, bs)]

        for s in range(slots):
            for i in range(rb):
                keep_ref[i, s] = result(i, q * slots + s)
                for m in range(1, n):
                    give_ref[m - 1, i, s] = result(i, lax.rem(q + m, n) * slots + s).astype(bf16)

    dense = [pltpu.VMEM((wide, width), bf16)]
    x0, x1 = send(low0, "rows", flip_x), send(low1, "rows", flip_x)
    c0, c1 = send(low0, "rows", flip_core), send(low1, "rows", flip_core)
    z0 = send(x0, "rows", move_z)
    (acc,) = call(cube_own, [lists, low0, low1, c0, c1, band], [acc_shape], dense)
    x1 = after(x1, acc)
    z1 = send(x1, "rows", move_z)
    cx0, cx1 = send(x0, "rows", core_x), send(x1, "rows", core_x)
    cz0 = send(z0, "rows", core_z)
    (acc,) = call(
        cube_near, [lists, acc, x0, x1, cx0, cx1, band], [acc_shape], dense, aliases={1: 0}
    )
    z1 = after(z1, acc)
    cz1 = send(z1, "rows", core_z)
    _, keep, give = call(
        cube_far,
        [lists, acc, z0, z1, cz0, cz1, band, square],
        [acc_shape, shape((rb, slots, part, bs), f32), shape((n - 1, rb, slots, part, bs), bf16)],
        dense,
        aliases={1: 0},
    )
    taken = received([send(nth(give, m - 1), "inner", shift(m)) for m in range(1, n)])

    def join(keep_ref, taken_ref, out_ref, turned):
        q = lax.axis_index("inner")
        for i in range(rb):
            for s in range(slots):
                turned[i, s, slice_at(q), :] = keep_ref[i, s]
                for m in range(1, n):
                    turned[i, s, slice_at(lax.rem(q - m + n, n)), :] = taken_ref[m - 1, i, s].astype(f32)
                out_ref[i, s] = turned[i, s].T

    (out,) = call(
        join,
        [keep, taken],
        [shape((rb, slots, bs, bs), f32)],
        [pltpu.VMEM((rb, slots, bs, bs), f32)],
        resident=False,
    )
    return out


def solution(mesh):
    in_specs = (P("rows", "inner", None, None), P(), P())
    out_specs = P("rows", "inner", None, None)
    return jax.shard_map(
        per_device, mesh=mesh, in_specs=in_specs, out_specs=out_specs, check_vma=False
    )
```

```python
import jax
import jax.numpy as jnp
from jax import lax
from jax.experimental import pallas as pl
from jax.experimental.pallas import tpu as pltpu
from jax.sharding import PartitionSpec as P

REACH = 2
BAND = 2 * REACH + 1
WIDE = 4 * REACH + 1
VMEM = pl.BlockSpec(memory_space=pltpu.VMEM)
SMEM = pl.BlockSpec(memory_space=pltpu.SMEM)
PARAMS = pltpu.CompilerParams(vmem_limit_bytes=16 * 1024 * 1024)


def call(kernel, ins, outs, scratch=(), aliases=None, resident=True):
    specs = [SMEM if x.dtype == jnp.int32 else VMEM for x in ins]
    if resident:
        outs = [pltpu.VMEM(x.shape, x.dtype) for x in outs]
    ins = [
        x if x.dtype == jnp.int32 else pltpu.with_memory_space_constraint(x, pltpu.VMEM)
        for x in ins
    ]
    return pl.pallas_call(
        kernel,
        out_shape=tuple(outs),
        in_specs=specs,
        out_specs=tuple(VMEM for _ in outs),
        scratch_shapes=list(scratch),
        input_output_aliases=aliases or {},
        compiler_params=PARAMS,
    )(*ins)


def after(x, *others):
    return lax.optimization_barrier((x, *others))[0]


def offsets(j):
    first = j < 2
    return {
        "own": 0,
        "x": jnp.where(first, 2, -2),
        "core": jnp.where(j % 2 == 0, 1, -1),
        "core_x": jnp.where(first, 1, -1),
        "z": jnp.where(first, -2, 2),
        "core_z": jnp.where(first, -1, 1),
    }


def per_device(p_blocks, col_lists, fill_lists):
    rb, slots, bs, _ = p_blocks.shape
    nb = col_lists.shape[0]
    fill = fill_lists.shape[1]
    n_rows = lax.axis_size("rows")
    n = lax.axis_size("inner")
    part = bs // n
    cuts = 2 if part % 32 == 0 else 1
    cols = part // cuts
    width = rb * bs
    bf16, f32 = jnp.bfloat16, jnp.float32
    shape = jax.ShapeDtypeStruct
    chunks = range(cuts)

    def shift(m):
        return [(i, (i + m) % n) for i in range(n)]

    def along(r):
        group, j = divmod(r, 4)
        return (group + (1 if j < 2 else -1)) % (n_rows // 4) * 4 + j

    flip_x = [(r, r ^ 2) for r in range(n_rows)]
    flip_core = [(r, r ^ 1) for r in range(n_rows)]
    move_z = [(r, along(r)) for r in range(n_rows)]

    def send(x, pairs, axis="rows"):
        return lax.ppermute(x, axis, pairs)

    def rows_at(index, size):
        return pl.ds(pl.multiple_of(index * size, size), size)

    def wrapped(x):
        return jnp.where(x < 0, x + nb, jnp.where(x >= nb, x - nb, x))

    def received(parts):
        return parts[0][None] if n == 2 else jnp.stack(parts)

    def nth(x, m):
        return x.reshape(x.shape[1:]) if n == 2 else x[m]

    def exchange(x):
        return received([send(nth(x, m - 1), shift(m), "inner") for m in range(1, n)])

    def pack(p_ref, mine_ref, *refs):
        own_refs, rest_refs, turned = refs[:cuts], refs[cuts : 2 * cuts], refs[-1]
        q = lax.axis_index("inner")
        for i in range(rb):
            for s in range(slots):
                turned[i, s] = p_ref[i, s].T
                mine_ref[i, s] = turned[i, s, rows_at(q, part), :]
                for c in chunks:
                    own_refs[c][i, s] = turned[i, s, rows_at(q * cuts + c, cols), :]
                    for m in range(1, n):
                        to = lax.rem(q + m, n)
                        rest_refs[c][m - 1, i, s] = turned[i, s, rows_at(to * cuts + c, cols), :]

    packed = call(
        pack,
        [p_blocks],
        [shape((rb, slots, part, bs), bf16)]
        + [shape((rb, slots, cols, bs), bf16)] * cuts
        + [shape((n - 1, rb, slots, cols, bs), bf16)] * cuts,
        [pltpu.VMEM((rb, slots, bs, bs), bf16)],
    )
    mine, own, rest = packed[0], packed[1 : 1 + cuts], packed[1 + cuts :]
    lists = jnp.concatenate([col_lists, fill_lists], axis=0)

    def add(ref, where, lanes, value):
        ref[where, lanes] = (ref[where, lanes].astype(f32) + value.astype(f32)).astype(bf16)

    def band_own(lists_ref, own_ref, *refs):
        rest_refs, out_ref = refs[:cuts], refs[cuts]
        o = lax.axis_index("rows")
        q = lax.axis_index("inner")
        out_ref[...] = jnp.zeros(out_ref.shape, bf16)
        for s in range(slots):
            for i in range(rb):
                c = wrapped(lists_ref[o * rb + i, q * slots + s] - rb * (o - REACH)) * n
                lanes = pl.ds(i * bs, bs)
                add(out_ref, rows_at(c + q, part), lanes, own_ref[i, s])
                for m in range(1, n):
                    at = (c + lax.rem(q + m, n)) * cuts
                    for k in chunks:
                        add(out_ref, rows_at(at + k, cols), lanes, rest_refs[k][m - 1, i, s])

    def band_other(lists_ref, in_ref, left_ref, *refs):
        got_refs, out_ref = refs[:cuts], refs[cuts]
        o = lax.axis_index("rows")
        q = lax.axis_index("inner")
        for s in range(slots):
            for i in range(rb):
                lanes = pl.ds(i * bs, bs)
                for m in range(1, n):
                    g = lax.rem(q - m + n, n)
                    c = wrapped(lists_ref[o * rb + i, g * slots + s] - rb * (o - REACH))
                    if n == 2:
                        for k in chunks:
                            at = (c * n + q) * cuts + k
                            add(out_ref, rows_at(at, cols), lanes, got_refs[k][0, i, s])
                        add(out_ref, rows_at(c * n + g, part), lanes, left_ref[i, s])
                    else:
                        add(out_ref, rows_at(c, bs), lanes, left_ref[g, i, s].T)

    band_shape = shape((BAND * width, width), bf16)
    (band,) = call(band_own, [lists, mine, *rest], [band_shape])

    got = [exchange(x) for x in rest]
    if n == 2:
        left = send(mine, shift(1), "inner")
    else:
        left = lax.all_gather(p_blocks, "inner", axis=0)
    c_mine = send(mine, flip_core)
    c_got = [send(x, flip_core) for x in got]
    x_own, x_got, z_own, z_got = [], [], [], []
    for c in chunks:
        x_own.append(send(own[c] if c == 0 else after(own[c], x_own[c - 1]), flip_x))
        x_got.append(send(got[c], flip_x))
        z_own.append(send(x_own[c], move_z))
        z_got.append(send(x_got[c], move_z))
    cx_own, cx_got = [send(x, flip_core) for x in x_own], [send(x, flip_core) for x in x_got]
    cz_own, cz_got = [send(x, flip_core) for x in z_own], [send(x, flip_core) for x in z_got]
    (band,) = call(band_other, [lists, band, left, *got], [band_shape], aliases={1: 0})

    span = BAND * rb * cols
    wide = WIDE * rb * cols
    acc_shape = shape((wide, width), f32)

    def weights(left_ref, d):
        return left_ref[rows_at(d + REACH, width), :]

    def square_term(lists_ref, d, own_ref, got_ref, left_ref, dense, acc_ref, first=False, cut=None):
        o = lax.axis_index("rows")
        q = lax.axis_index("inner")
        source = lax.rem(o + d + n_rows, n_rows)
        dense[...] = jnp.zeros(dense.shape, bf16)

        def place(k, slot, value):
            c = wrapped(lists_ref[source * rb + k, slot] - rb * (source - REACH))
            add(dense, rows_at(c, cols), pl.ds(k * bs, bs), value)

        for s in range(slots):
            for k in range(rb):
                value = own_ref[k, s] if cut is None else own_ref[k, s, pl.ds(cut * cols, cols), :]
                place(k, q * slots + s, value)
                for m in range(1, n):
                    place(k, lax.rem(q - m + n, n) * slots + s, got_ref[m - 1, k, s])
        term = jnp.dot(dense[...], weights(left_ref, d), preferred_element_type=f32)
        where = pl.ds(pl.multiple_of((d + REACH) * rb * cols, rb * cols), span)
        if first:
            acc_ref[...] = jnp.zeros(acc_ref.shape, f32)
            acc_ref[where, :] = term
        else:
            acc_ref[where, :] += term

    def kept(lists_ref, i, v):
        o = lax.axis_index("rows")
        return rows_at(wrapped(lists_ref[nb + o * rb + i, v] - rb * (o - 2 * REACH)), cols)

    def square(c, band):
        def near(lists_ref, w, wg, u, ug, x, xg, cx, cxg, left_ref, acc_ref, dense):
            j = lax.rem(lax.axis_index("rows"), 4)
            d = offsets(j)
            square_term(lists_ref, 0, w, wg, left_ref, dense, acc_ref, first=True)
            square_term(lists_ref, d["core"], u, ug, left_ref, dense, acc_ref, cut=c)
            square_term(lists_ref, d["x"], x, xg, left_ref, dense, acc_ref)

            @pl.when((j == 1) | (j == 2))
            def _():
                square_term(lists_ref, d["core_x"], cx, cxg, left_ref, dense, acc_ref)

        def far(lists_ref, acc_in, z, zg, cz, czg, left_ref, acc_ref, sq_ref, low_ref, dense):
            j = lax.rem(lax.axis_index("rows"), 4)
            d = offsets(j)
            square_term(lists_ref, d["z"], z, zg, left_ref, dense, acc_ref)

            @pl.when((j == 0) | (j == 3))
            def _():
                square_term(lists_ref, d["core_z"], cz, czg, left_ref, dense, acc_ref)

            for v in range(fill):
                for i in range(rb):
                    value = acc_ref[kept(lists_ref, i, v), pl.ds(i * bs, bs)]
                    sq_ref[i, v] = value
                    low_ref[i, v] = value.astype(bf16)

        dense = [pltpu.VMEM((span, width), bf16)]
        (acc,) = call(
            near,
            [lists, own[c], got[c], c_mine, c_got[c], x_own[c], x_got[c], cx_own[c], cx_got[c], band],
            [acc_shape],
            dense,
        )
        kept_shape = (rb, fill, cols, bs)
        return call(
            far,
            [lists, acc, z_own[c], z_got[c], cz_own[c], cz_got[c], band],
            [acc_shape, shape(kept_shape, f32), shape(kept_shape, bf16)],
            dense,
            aliases={1: 0},
        )[1:]

    def cube_term(lists_ref, d, reach, low_ref, left_ref, dense, acc_ref, first=False):
        o = lax.axis_index("rows")
        source = lax.rem(o + d + n_rows, n_rows)
        blocks = (WIDE - reach) * rb
        start = jnp.maximum(d, 0) * rb
        rows = blocks * cols
        dense[:rows, :] = jnp.zeros((rows, width), bf16)
        for v in range(fill):
            for k in range(rb):
                c = wrapped(lists_ref[nb + source * rb + k, v] - rb * (o - 2 * REACH)) - start

                @pl.when((c >= 0) & (c < blocks))
                def _():
                    dense[rows_at(c, cols), pl.ds(k * bs, bs)] = low_ref[k, v]

        term = jnp.dot(dense[:rows, :], weights(left_ref, d), preferred_element_type=f32)
        if first:
            acc_ref[...] = term
        else:
            acc_ref[pl.ds(pl.multiple_of(start * cols, rb * cols), rows), :] += term

    def cube_own(lists_ref, w, u, left_ref, acc_ref, dense):
        d = offsets(lax.rem(lax.axis_index("rows"), 4))
        cube_term(lists_ref, 0, 0, w, left_ref, dense, acc_ref, first=True)
        cube_term(lists_ref, d["core"], 1, u, left_ref, dense, acc_ref)

    def cube_near(lists_ref, acc_in, x, cx, left_ref, acc_ref, dense):
        j = lax.rem(lax.axis_index("rows"), 4)
        d = offsets(j)
        cube_term(lists_ref, d["x"], 2, x, left_ref, dense, acc_ref)

        @pl.when((j == 1) | (j == 2))
        def _():
            cube_term(lists_ref, d["core_x"], 1, cx, left_ref, dense, acc_ref)

    def cube_far(lists_ref, acc_in, z, cz, left_ref, sq_ref, acc_ref, keep_ref, give_ref, dense):
        q = lax.axis_index("inner")
        j = lax.rem(lax.axis_index("rows"), 4)
        d = offsets(j)
        cube_term(lists_ref, d["z"], 2, z, left_ref, dense, acc_ref)

        @pl.when((j == 0) | (j == 3))
        def _():
            cube_term(lists_ref, d["core_z"], 1, cz, left_ref, dense, acc_ref)

        def result(i, v):
            return 3.0 * sq_ref[i, v] - 2.0 * acc_ref[kept(lists_ref, i, v), pl.ds(i * bs, bs)]

        for s in range(slots):
            for i in range(rb):
                keep_ref[i, s] = result(i, q * slots + s)
                for m in range(1, n):
                    give_ref[m - 1, i, s] = result(i, lax.rem(q + m, n) * slots + s).astype(bf16)

    def cube(sq, low, x, z, ahead):
        dense = [pltpu.VMEM((wide, width), bf16)]
        u, cx, cz = send(low, flip_core), send(x, flip_core), send(z, flip_core)
        (acc,) = call(cube_own, [lists, low, u, after(band, *ahead)], [acc_shape], dense)
        (acc,) = call(cube_near, [lists, acc, x, cx, band], [acc_shape], dense, aliases={1: 0})
        return call(
            cube_far,
            [lists, acc, z, cz, band, sq],
            [acc_shape, shape((rb, slots, cols, bs), f32), shape((n - 1, rb, slots, cols, bs), bf16)],
            dense,
            aliases={1: 0},
        )[1:]

    sq, low = [], []
    for c in chunks:
        one = square(c, after(band, *low))
        sq.append(one[0])
        low.append(one[1])
    x = [send(v, flip_x) for v in low]
    z = [send(v, move_z) for v in x]
    keep, give = [], []
    for c in chunks:
        one = cube(sq[c], low[c], x[c], z[c], [low[-1]] + give)
        keep.append(one[0])
        give.append(one[1])
    taken = [exchange(v) for v in give]

    def join(*refs):
        keep_refs, taken_refs, out_ref, turned = refs[:cuts], refs[cuts : 2 * cuts], refs[-2], refs[-1]
        q = lax.axis_index("inner")
        for i in range(rb):
            for s in range(slots):
                for c in chunks:
                    turned[i, s, rows_at(q * cuts + c, cols), :] = keep_refs[c][i, s]
                    for m in range(1, n):
                        at = lax.rem(q - m + n, n) * cuts + c
                        turned[i, s, rows_at(at, cols), :] = taken_refs[c][m - 1, i, s].astype(f32)
                out_ref[i, s] = turned[i, s].T

    (out,) = call(
        join,
        [*keep, *taken],
        [shape((rb, slots, bs, bs), f32)],
        [pltpu.VMEM((rb, slots, bs, bs), f32)],
        resident=False,
    )
    return out


def solution(mesh):
    in_specs = (P("rows", "inner", None, None), P(), P())
    out_specs = P("rows", "inner", None, None)
    return jax.shard_map(
        per_device, mesh=mesh, in_specs=in_specs, out_specs=out_specs, check_vma=False
    )
```

```python
import jax
import jax.numpy as jnp
from jax import lax
from jax.experimental import pallas as pl
from jax.experimental.pallas import tpu as pltpu
from jax.sharding import PartitionSpec as P

REACH = 2
BAND = 2 * REACH + 1
WIDE = 4 * REACH + 1
VMEM = pl.BlockSpec(memory_space=pltpu.VMEM)
SMEM = pl.BlockSpec(memory_space=pltpu.SMEM)
PARAMS = pltpu.CompilerParams(vmem_limit_bytes=16 * 1024 * 1024)


def call(kernel, ins, outs, scratch=(), aliases=None, resident=True, us=3):
    specs = [SMEM if x.dtype == jnp.int32 else VMEM for x in ins]
    if resident:
        outs = [pltpu.VMEM(x.shape, x.dtype) for x in outs]
    ins = [
        x if x.dtype == jnp.int32 else pltpu.with_memory_space_constraint(x, pltpu.VMEM)
        for x in ins
    ]
    return pl.pallas_call(
        kernel,
        out_shape=tuple(outs),
        in_specs=specs,
        out_specs=tuple(VMEM for _ in outs),
        scratch_shapes=list(scratch),
        input_output_aliases=aliases or {},
        compiler_params=PARAMS,
    )(*ins)


def after(x, *others):
    return lax.optimization_barrier((x, *others))[0]


def offsets(j):
    first = j < 2
    return {
        "own": 0,
        "x": jnp.where(first, 2, -2),
        "core": jnp.where(j % 2 == 0, 1, -1),
        "core_x": jnp.where(first, 1, -1),
        "z": jnp.where(first, -2, 2),
        "core_z": jnp.where(first, -1, 1),
    }


def per_device(p_blocks, col_lists, fill_lists):
    rb, slots, bs, _ = p_blocks.shape
    nb = col_lists.shape[0]
    fill = fill_lists.shape[1]
    n_rows = lax.axis_size("rows")
    n = lax.axis_size("inner")
    part = bs // n
    cuts = 2 if part % 32 == 0 else 1
    cols = part // cuts
    width = rb * bs
    bf16, f32 = jnp.bfloat16, jnp.float32
    shape = jax.ShapeDtypeStruct
    chunks = range(cuts)

    def shift(m):
        return [(i, (i + m) % n) for i in range(n)]

    def along(r):
        group, j = divmod(r, 4)
        return (group + (1 if j < 2 else -1)) % (n_rows // 4) * 4 + j

    flip_x = [(r, r ^ 2) for r in range(n_rows)]
    flip_core = [(r, r ^ 1) for r in range(n_rows)]
    move_z = [(r, along(r)) for r in range(n_rows)]

    def send(x, pairs, axis="rows"):
        return lax.ppermute(x, axis, pairs)

    def rows_at(index, size):
        return pl.ds(pl.multiple_of(index * size, size), size)

    def wrapped(x):
        return jnp.where(x < 0, x + nb, jnp.where(x >= nb, x - nb, x))

    def received(parts):
        return parts[0][None] if n == 2 else jnp.stack(parts)

    def nth(x, m):
        return x.reshape(x.shape[1:]) if n == 2 else x[m]

    def exchange(x):
        return received([send(nth(x, m - 1), shift(m), "inner") for m in range(1, n)])

    def pack(p_ref, mine_ref, *refs):
        rest_refs, turned = refs[:cuts], refs[-1]
        q = lax.axis_index("inner")
        for i in range(rb):
            for s in range(slots):
                turned[i, s] = p_ref[i, s].T
                mine_ref[i, s] = turned[i, s, rows_at(q, part), :]
                for c in chunks:
                    for m in range(1, n):
                        to = lax.rem(q + m, n)
                        rest_refs[c][m - 1, i, s] = turned[i, s, rows_at(to * cuts + c, cols), :]

    packed = call(
        pack,
        [p_blocks],
        [shape((rb, slots, part, bs), bf16)]
        + [shape((n - 1, rb, slots, cols, bs), bf16)] * cuts,
        [pltpu.VMEM((rb, slots, bs, bs), bf16)],
        us=1,
    )
    mine, rest = packed[0], packed[1:]
    lists = jnp.concatenate([col_lists.T, fill_lists.T], axis=1)

    def add(ref, where, lanes, value):
        ref[where, lanes] = (ref[where, lanes].astype(f32) + value.astype(f32)).astype(bf16)

    def column(lists_ref, i, slot):
        o = lax.axis_index("rows")
        return wrapped(lists_ref[slot, o * rb + i] - rb * (o - REACH))

    def start_rows(lists_ref, mine_ref, *refs):
        out_refs = refs[:cuts]
        q = lax.axis_index("inner")
        for c in chunks:
            out_refs[c][...] = jnp.zeros(out_refs[c].shape, bf16)
        for s in range(slots):
            for i in range(rb):
                at = column(lists_ref, i, q * slots + s)
                for c in chunks:
                    value = mine_ref[i, s, pl.ds(c * cols, cols), :]
                    add(out_refs[c], rows_at(at, cols), pl.ds(i * bs, bs), value)

    def start_band(lists_ref, *refs):
        rest_refs, out_ref = refs[:cuts], refs[-1]
        q = lax.axis_index("inner")
        out_ref[...] = jnp.zeros(out_ref.shape, bf16)
        for s in range(slots):
            for i in range(rb):
                at = column(lists_ref, i, q * slots + s) * n + lax.rem(q + 1, n)
                for c in chunks:
                    value = rest_refs[c][0, i, s]
                    add(out_ref, rows_at(at * cuts + c, cols), pl.ds(i * bs, bs), value)

    def end_rows(lists_ref, in_ref, got_ref, out_ref):
        q = lax.axis_index("inner")
        for s in range(slots):
            for i in range(rb):
                for m in range(1, n):
                    at = column(lists_ref, i, lax.rem(q - m + n, n) * slots + s)
                    add(out_ref, rows_at(at, cols), pl.ds(i * bs, bs), got_ref[m - 1, i, s])

    def end_band(lists_ref, in_ref, left_ref, *refs):
        dense_refs, out_ref = refs[:cuts], refs[-1]
        q = lax.axis_index("inner")
        other = lax.rem(q + 1, n)
        for s in range(slots):
            for i in range(rb):
                at = column(lists_ref, i, other * slots + s) * n + other
                add(out_ref, rows_at(at, part), pl.ds(i * bs, bs), left_ref[i, s])
        for k in range(BAND * rb):
            for c in chunks:
                out_ref[rows_at((k * n + q) * cuts + c, cols), :] = dense_refs[c][pl.ds(k * cols, cols), :]

    def whole_band(lists_ref, left_ref, out_ref):
        out_ref[...] = jnp.zeros(out_ref.shape, bf16)
        for g in range(n):
            for s in range(slots):
                for i in range(rb):
                    at = column(lists_ref, i, g * slots + s)
                    add(out_ref, rows_at(at, bs), pl.ds(i * bs, bs), left_ref[g, i, s].T)

    span = BAND * rb * cols
    wide = WIDE * rb * cols
    acc_shape = shape((wide, width), f32)
    rows_shape = shape((span, width), bf16)
    band_shape = shape((BAND * width, width), bf16)
    own = call(start_rows, [lists, mine], [rows_shape] * cuts, us=1)
    got = [exchange(x) for x in rest]
    if n == 2:
        (band,) = call(start_band, [lists, *rest], [band_shape], us=1)
        left = send(after(mine, got[0]), shift(1), "inner")
    else:
        left = lax.all_gather(p_blocks, "inner", axis=0)
    own = [
        call(end_rows, [lists, own[c], got[c]], [rows_shape], aliases={1: 0}, us=1)[0]
        for c in chunks
    ]
    if n == 2:
        (band,) = call(end_band, [lists, band, left, *own], [band_shape], aliases={1: 0}, us=2)
    else:
        (band,) = call(whole_band, [lists, left], [band_shape], us=2)

    def moved(v):
        x = send(v, flip_x)
        return x, send(x, move_z)

    def weights(left_ref, d):
        return left_ref[rows_at(d + REACH, width), :]

    def square_term(d, rows_ref, left_ref, acc_ref):
        term = jnp.dot(rows_ref[...], weights(left_ref, d), preferred_element_type=f32)
        where = pl.ds(pl.multiple_of((d + REACH) * rb * cols, rb * cols), span)
        acc_ref[where, :] += term

    def square_near(w, u, x, cx, left_ref, acc_ref):
        j = lax.rem(lax.axis_index("rows"), 4)
        d = offsets(j)
        edge = REACH * rb * cols
        acc_ref[:edge, :] = jnp.zeros((edge, width), f32)
        acc_ref[edge : edge + span, :] = jnp.dot(
            w[...], left_ref[REACH * width : (REACH + 1) * width, :], preferred_element_type=f32
        )
        acc_ref[edge + span :, :] = jnp.zeros((edge, width), f32)
        square_term(d["core"], u, left_ref, acc_ref)
        square_term(d["x"], x, left_ref, acc_ref)

        @pl.when((j == 1) | (j == 2))
        def _():
            square_term(d["core_x"], cx, left_ref, acc_ref)

    def square_far(lists_ref, acc_in, z, cz, left_ref, acc_ref, sq_ref, low_ref):
        j = lax.rem(lax.axis_index("rows"), 4)
        d = offsets(j)
        square_term(d["z"], z, left_ref, acc_ref)

        @pl.when((j == 0) | (j == 3))
        def _():
            square_term(d["core_z"], cz, left_ref, acc_ref)

        for v in range(fill):
            for i in range(rb):
                value = acc_ref[kept(lists_ref, i, v), pl.ds(i * bs, bs)]
                sq_ref[i, v] = value
                low_ref[i, v] = value.astype(bf16)

    kept_shape = (rb, fill, cols, bs)

    def square(w, x, z, lead):
        u, cx = send(w, flip_core), send(x, flip_core)
        (acc,) = call(square_near, [after(w, *lead), u, x, cx, band], [acc_shape], us=2)
        z = after(z, acc)
        return call(
            square_far,
            [lists, acc, z, send(z, flip_core), band],
            [acc_shape, shape(kept_shape, f32), shape(kept_shape, bf16)],
            aliases={1: 0},
            us=2,
        )[1:]

    def kept(lists_ref, i, v):
        o = lax.axis_index("rows")
        return rows_at(wrapped(lists_ref[v, nb + o * rb + i] - rb * (o - 2 * REACH)), cols)

    def cube_term(lists_ref, d, reach, low_ref, left_ref, dense, acc_ref, first=False):
        o = lax.axis_index("rows")
        source = lax.rem(o + d + n_rows, n_rows)
        blocks = (WIDE - reach) * rb
        start = jnp.maximum(d, 0) * rb
        rows = blocks * cols
        dense[:rows, :] = jnp.zeros((rows, width), bf16)
        for v in range(fill):
            for k in range(rb):
                c = wrapped(lists_ref[v, nb + source * rb + k] - rb * (o - 2 * REACH)) - start
                c = jnp.where((c >= 0) & (c < blocks), c, blocks)
                dense[rows_at(c, cols), pl.ds(k * bs, bs)] = low_ref[k, v]

        term = jnp.dot(dense[:rows, :], weights(left_ref, d), preferred_element_type=f32)
        if first:
            acc_ref[...] = term
        else:
            acc_ref[pl.ds(pl.multiple_of(start * cols, rb * cols), rows), :] += term

    def cube_own(lists_ref, w, u, left_ref, acc_ref, dense):
        d = offsets(lax.rem(lax.axis_index("rows"), 4))
        cube_term(lists_ref, 0, 0, w, left_ref, dense, acc_ref, first=True)
        cube_term(lists_ref, d["core"], 1, u, left_ref, dense, acc_ref)

    def cube_near(lists_ref, acc_in, x, cx, left_ref, acc_ref, dense):
        j = lax.rem(lax.axis_index("rows"), 4)
        d = offsets(j)
        cube_term(lists_ref, d["x"], 2, x, left_ref, dense, acc_ref)

        @pl.when((j == 1) | (j == 2))
        def _():
            cube_term(lists_ref, d["core_x"], 1, cx, left_ref, dense, acc_ref)

    def cube_far(lists_ref, acc_in, z, cz, left_ref, sq_ref, acc_ref, keep_ref, give_ref, dense):
        q = lax.axis_index("inner")
        j = lax.rem(lax.axis_index("rows"), 4)
        d = offsets(j)
        cube_term(lists_ref, d["z"], 2, z, left_ref, dense, acc_ref)

        @pl.when((j == 0) | (j == 3))
        def _():
            cube_term(lists_ref, d["core_z"], 1, cz, left_ref, dense, acc_ref)

        def result(i, v):
            return 3.0 * sq_ref[i, v] - 2.0 * acc_ref[kept(lists_ref, i, v), pl.ds(i * bs, bs)]

        for s in range(slots):
            for i in range(rb):
                keep_ref[i, s] = result(i, q * slots + s)
                for m in range(1, n):
                    give_ref[m - 1, i, s] = result(i, lax.rem(q + m, n) * slots + s).astype(bf16)

    dense = [pltpu.VMEM((wide + cols, width), bf16)]
    x, z, sq, low, x2, z2 = [], [], [], [], [], []
    for c in chunks:
        x_c, z_c = moved(own[c])
        one = square(own[c], x_c, z_c, low)
        sq.append(one[0])
        low.append(one[1])
    keep, give, near = [], [], []
    for c in chunks:
        x_c = send(low[c], flip_x)
        u = send(low[c], flip_core)
        (acc,) = call(
            cube_own, [lists, low[c], u, after(band, low[-1], *near)], [acc_shape], dense, us=3
        )
        x2.append(x_c)
        z2.append(send(x_c, move_z))
        cx = send(x_c, flip_core)
        (acc,) = call(cube_near, [lists, acc, x_c, cx, band], [acc_shape], dense, aliases={1: 0}, us=2)
        near.append(acc)
    for c in chunks:
        z_c = after(z2[c], near[c], *give)
        one = call(
            cube_far,
            [lists, near[c], z_c, send(z_c, flip_core), band, sq[c]],
            [acc_shape, shape((rb, slots, cols, bs), f32), shape((n - 1, rb, slots, cols, bs), bf16)],
            dense,
            aliases={1: 0},
            us=3,
        )[1:]
        keep.append(one[0])
        give.append(one[1])
    taken = [exchange(v) for v in give]

    def join(*refs):
        keep_refs, taken_refs, out_ref, turned = refs[:cuts], refs[cuts : 2 * cuts], refs[-2], refs[-1]
        q = lax.axis_index("inner")
        for i in range(rb):
            for s in range(slots):
                for c in chunks:
                    turned[i, s, rows_at(q * cuts + c, cols), :] = keep_refs[c][i, s]
                    for m in range(1, n):
                        at = lax.rem(q - m + n, n) * cuts + c
                        turned[i, s, rows_at(at, cols), :] = taken_refs[c][m - 1, i, s].astype(f32)
                out_ref[i, s] = turned[i, s].T

    (out,) = call(
        join,
        [*keep, *taken],
        [shape((rb, slots, bs, bs), f32)],
        [pltpu.VMEM((rb, slots, bs, bs), f32)],
        resident=False,
    )
    return out


def solution(mesh):
    in_specs = (P("rows", "inner", None, None), P(), P())
    out_specs = P("rows", "inner", None, None)
    return jax.shard_map(
        per_device, mesh=mesh, in_specs=in_specs, out_specs=out_specs, check_vma=False
    )
```

```python
import jax
import jax.numpy as jnp
from jax import lax
from jax.experimental import pallas as pl
from jax.experimental.pallas import tpu as pltpu
from jax.sharding import PartitionSpec as P

REACH = 2
BAND = 2 * REACH + 1
WIDE = 4 * REACH + 1
VMEM = pl.BlockSpec(memory_space=pltpu.VMEM)
HBM = pl.BlockSpec(memory_space=pltpu.HBM)
SMEM = pl.BlockSpec(memory_space=pltpu.SMEM)
PARAMS = pltpu.CompilerParams(vmem_limit_bytes=16 * 1024 * 1024)


def call(kernel, ins, outs, scratch=(), aliases=None, hbm_in=False, hbm_out=False):
    here = HBM if hbm_in else VMEM
    specs = [SMEM if x.dtype == jnp.int32 else here for x in ins]
    if not hbm_out:
        outs = [pltpu.VMEM(x.shape, x.dtype) for x in outs]
    place = pltpu.HBM if hbm_in else pltpu.VMEM
    ins = [
        x if x.dtype == jnp.int32 else pltpu.with_memory_space_constraint(x, place) for x in ins
    ]
    return pl.pallas_call(
        kernel,
        out_shape=tuple(outs),
        in_specs=specs,
        out_specs=tuple(HBM if hbm_out else VMEM for _ in outs),
        scratch_shapes=list(scratch),
        input_output_aliases=aliases or {},
        compiler_params=PARAMS,
    )(*ins)


def after(x, *others):
    return lax.optimization_barrier((x, *others))[0]


def offsets(j):
    first = j < 2
    return {
        "own": 0,
        "x": jnp.where(first, 2, -2),
        "core": jnp.where(j % 2 == 0, 1, -1),
        "core_x": jnp.where(first, 1, -1),
        "z": jnp.where(first, -2, 2),
        "core_z": jnp.where(first, -1, 1),
    }


def per_device(p_blocks, col_lists, fill_lists):
    rb, slots, bs, _ = p_blocks.shape
    nb = col_lists.shape[0]
    fill = fill_lists.shape[1]
    n_rows = lax.axis_size("rows")
    n = lax.axis_size("inner")
    part = bs // n
    sizes = [part // 2] * 2 if part % 32 == 0 else [part]
    cuts = len(sizes)
    offs = [sum(sizes[:c]) for c in range(cuts)]
    unit = min(sizes)
    width = rb * bs
    bf16, f32 = jnp.bfloat16, jnp.float32
    shape = jax.ShapeDtypeStruct
    chunks = range(cuts)

    def shift(m):
        return [(i, (i + m) % n) for i in range(n)]

    def along(r):
        group, j = divmod(r, 4)
        return (group + (1 if j < 2 else -1)) % (n_rows // 4) * 4 + j

    flip_x = [(r, r ^ 2) for r in range(n_rows)]
    flip_core = [(r, r ^ 1) for r in range(n_rows)]
    move_z = [(r, along(r)) for r in range(n_rows)]

    def send(x, pairs, axis="rows"):
        return lax.ppermute(x, axis, pairs)

    def rows_at(index, size):
        return pl.ds(pl.multiple_of(index * size, size), size)

    def piece(index, c):
        return pl.ds(pl.multiple_of(index * part + offs[c], unit), sizes[c])

    def wrapped(x):
        return jnp.where(x < 0, x + nb, jnp.where(x >= nb, x - nb, x))

    def received(parts):
        return parts[0][None] if n == 2 else jnp.stack(parts)

    def nth(x, m):
        return x.reshape(x.shape[1:]) if n == 2 else x[m]

    def exchange(x):
        return received([send(nth(x, m - 1), shift(m), "inner") for m in range(1, n)])

    def pack(p_ref, mine_ref, *refs):
        rest_refs, (raw, turned, sems) = refs[:cuts], refs[-3:]
        q = lax.axis_index("inner")
        copies = [pltpu.make_async_copy(p_ref.at[i], raw.at[i], sems.at[i]) for i in range(rb)]
        for copy in copies:
            copy.start()
        for i in range(rb):
            copies[i].wait()
            for s in range(slots):
                turned[i, s] = raw[i, s].T
                mine_ref[i, s] = turned[i, s, rows_at(q, part), :]
                for c in chunks:
                    for m in range(1, n):
                        rest_refs[c][m - 1, i, s] = turned[i, s, piece(lax.rem(q + m, n), c), :]

    whole = pltpu.VMEM((rb, slots, bs, bs), bf16)
    packed = call(
        pack,
        [p_blocks],
        [shape((rb, slots, part, bs), bf16)]
        + [shape((n - 1, rb, slots, k, bs), bf16) for k in sizes],
        [whole, whole, pltpu.SemaphoreType.DMA((rb,))],
        hbm_in=True,
    )
    mine, rest = packed[0], packed[1:]
    lists = jnp.concatenate([col_lists.T, fill_lists.T], axis=1)

    def add(ref, where, lanes, value):
        ref[where, lanes] = (ref[where, lanes].astype(f32) + value.astype(f32)).astype(bf16)

    def column(lists_ref, i, slot):
        o = lax.axis_index("rows")
        return wrapped(lists_ref[slot, o * rb + i] - rb * (o - REACH))

    def start_rows(lists_ref, mine_ref, *refs):
        out_refs = refs[:cuts]
        q = lax.axis_index("inner")
        for c in chunks:
            out_refs[c][...] = jnp.zeros(out_refs[c].shape, bf16)
        for s in range(slots):
            for i in range(rb):
                at = column(lists_ref, i, q * slots + s)
                for c in chunks:
                    value = mine_ref[i, s, pl.ds(offs[c], sizes[c]), :]
                    add(out_refs[c], rows_at(at, sizes[c]), pl.ds(i * bs, bs), value)

    def start_band(lists_ref, *refs):
        rest_refs, out_ref = refs[:cuts], refs[-1]
        q = lax.axis_index("inner")
        out_ref[...] = jnp.zeros(out_ref.shape, bf16)
        for s in range(slots):
            for i in range(rb):
                at = column(lists_ref, i, q * slots + s) * n + lax.rem(q + 1, n)
                for c in chunks:
                    value = rest_refs[c][0, i, s]
                    add(out_ref, piece(at, c), pl.ds(i * bs, bs), value)

    def end_rows(lists_ref, in_ref, got_ref, out_ref):
        q = lax.axis_index("inner")
        for s in range(slots):
            for i in range(rb):
                for m in range(1, n):
                    at = column(lists_ref, i, lax.rem(q - m + n, n) * slots + s)
                    add(out_ref, rows_at(at, got_ref.shape[3]), pl.ds(i * bs, bs), got_ref[m - 1, i, s])

    def end_band(lists_ref, in_ref, left_ref, *refs):
        dense_refs, out_ref = refs[:cuts], refs[-1]
        q = lax.axis_index("inner")
        other = lax.rem(q + 1, n)
        for s in range(slots):
            for i in range(rb):
                at = column(lists_ref, i, other * slots + s) * n + other
                add(out_ref, rows_at(at, part), pl.ds(i * bs, bs), left_ref[i, s])
        for k in range(BAND * rb):
            for c in chunks:
                out_ref[piece(k * n + q, c), :] = dense_refs[c][pl.ds(k * sizes[c], sizes[c]), :]

    def whole_band(lists_ref, left_ref, out_ref):
        out_ref[...] = jnp.zeros(out_ref.shape, bf16)
        for g in range(n):
            for s in range(slots):
                for i in range(rb):
                    at = column(lists_ref, i, g * slots + s)
                    add(out_ref, rows_at(at, bs), pl.ds(i * bs, bs), left_ref[g, i, s].T)

    band_shape = shape((BAND * width, width), bf16)
    rows_shapes = [shape((BAND * rb * k, width), bf16) for k in sizes]
    acc_shapes = [shape((WIDE * rb * k, width), f32) for k in sizes]
    own = call(start_rows, [lists, mine], rows_shapes)
    got = [exchange(x) for x in rest]
    if n == 2:
        (band,) = call(start_band, [lists, *rest], [band_shape])
        left = send(after(mine, got[0]), shift(1), "inner")
    else:
        left = lax.all_gather(p_blocks, "inner", axis=0)
    own = [
        call(end_rows, [lists, own[c], got[c]], [rows_shapes[c]], aliases={1: 0})[0]
        for c in chunks
    ]
    if n == 2:
        (band,) = call(end_band, [lists, band, left, *own], [band_shape], aliases={1: 0})
    else:
        (band,) = call(whole_band, [lists, left], [band_shape])

    def moved(v, *first):
        x = send(v, flip_x)
        return x, send(after(x, *first), move_z)

    def weights(left_ref, d):
        return left_ref[rows_at(d + REACH, width), :]

    def square_term(d, rows_ref, left_ref, acc_ref):
        term = jnp.dot(rows_ref[...], weights(left_ref, d), preferred_element_type=f32)
        span = rows_ref.shape[0]
        step = span // BAND
        acc_ref[pl.ds(pl.multiple_of((d + REACH) * step, step), span), :] += term

    def square_near(w, u, x, cx, left_ref, acc_ref):
        j = lax.rem(lax.axis_index("rows"), 4)
        d = offsets(j)
        span = w.shape[0]
        edge = span // BAND * REACH
        acc_ref[:edge, :] = jnp.zeros((edge, width), f32)
        acc_ref[edge : edge + span, :] = jnp.dot(
            w[...], left_ref[REACH * width : (REACH + 1) * width, :], preferred_element_type=f32
        )
        acc_ref[edge + span :, :] = jnp.zeros((edge, width), f32)
        square_term(d["core"], u, left_ref, acc_ref)
        square_term(d["x"], x, left_ref, acc_ref)

        @pl.when((j == 1) | (j == 2))
        def _():
            square_term(d["core_x"], cx, left_ref, acc_ref)

    def square_far(lists_ref, acc_in, z, cz, left_ref, acc_ref, sq_ref, low_ref):
        j = lax.rem(lax.axis_index("rows"), 4)
        d = offsets(j)
        square_term(d["z"], z, left_ref, acc_ref)

        @pl.when((j == 0) | (j == 3))
        def _():
            square_term(d["core_z"], cz, left_ref, acc_ref)

        for v in range(fill):
            for i in range(rb):
                value = acc_ref[kept(lists_ref, i, v, sq_ref.shape[2]), pl.ds(i * bs, bs)]
                sq_ref[i, v] = value
                low_ref[i, v] = value.astype(bf16)

    def square(c, w, x, z, lead):
        kept_shape, acc_shape = (rb, fill, sizes[c], bs), acc_shapes[c]
        u, cx = send(w, flip_core), send(x, flip_core)
        (acc,) = call(square_near, [after(w, *lead), u, x, cx, band], [acc_shape])
        z = after(z, acc)
        return call(
            square_far,
            [lists, acc, z, send(z, flip_core), band],
            [acc_shape, shape(kept_shape, f32), shape(kept_shape, bf16)],
            aliases={1: 0},
        )[1:]

    def kept(lists_ref, i, v, cols):
        o = lax.axis_index("rows")
        return rows_at(wrapped(lists_ref[v, nb + o * rb + i] - rb * (o - 2 * REACH)), cols)

    def cube_term(lists_ref, d, reach, low_ref, left_ref, dense, acc_ref, first=False):
        o = lax.axis_index("rows")
        source = lax.rem(o + d + n_rows, n_rows)
        blocks = (WIDE - reach) * rb
        cols = low_ref.shape[2]
        start = jnp.maximum(d, 0) * rb
        rows = blocks * cols
        dense[:rows, :] = jnp.zeros((rows, width), bf16)
        for v in range(fill):
            for k in range(rb):
                c = wrapped(lists_ref[v, nb + source * rb + k] - rb * (o - 2 * REACH)) - start
                c = jnp.where((c >= 0) & (c < blocks), c, blocks)
                dense[rows_at(c, cols), pl.ds(k * bs, bs)] = low_ref[k, v]

        term = jnp.dot(dense[:rows, :], weights(left_ref, d), preferred_element_type=f32)
        if first:
            acc_ref[...] = term
        else:
            acc_ref[pl.ds(pl.multiple_of(start * cols, rb * cols), rows), :] += term

    def cube_own(lists_ref, w, u, left_ref, acc_ref, dense):
        d = offsets(lax.rem(lax.axis_index("rows"), 4))
        cube_term(lists_ref, 0, 0, w, left_ref, dense, acc_ref, first=True)
        cube_term(lists_ref, d["core"], 1, u, left_ref, dense, acc_ref)

    def cube_near(lists_ref, acc_in, x, cx, left_ref, acc_ref, dense):
        j = lax.rem(lax.axis_index("rows"), 4)
        d = offsets(j)
        cube_term(lists_ref, d["x"], 2, x, left_ref, dense, acc_ref)

        @pl.when((j == 1) | (j == 2))
        def _():
            cube_term(lists_ref, d["core_x"], 1, cx, left_ref, dense, acc_ref)

    def cube_far(lists_ref, acc_in, z, cz, left_ref, sq_ref, acc_ref, keep_ref, give_ref, dense):
        q = lax.axis_index("inner")
        j = lax.rem(lax.axis_index("rows"), 4)
        d = offsets(j)
        cube_term(lists_ref, d["z"], 2, z, left_ref, dense, acc_ref)

        @pl.when((j == 0) | (j == 3))
        def _():
            cube_term(lists_ref, d["core_z"], 1, cz, left_ref, dense, acc_ref)

        def result(i, v):
            return 3.0 * sq_ref[i, v] - 2.0 * acc_ref[kept(lists_ref, i, v, sq_ref.shape[2]), pl.ds(i * bs, bs)]

        for s in range(slots):
            for i in range(rb):
                keep_ref[i, s] = result(i, q * slots + s)
                for m in range(1, n):
                    give_ref[m - 1, i, s] = result(i, lax.rem(q + m, n) * slots + s).astype(bf16)

    dense = [[pltpu.VMEM(((WIDE * rb + 1) * k, width), bf16)] for k in sizes]
    x, z, sq, low, x2, z2 = [], [], [], [], [], []
    for c in chunks:
        x_c, z_c = moved(own[c], *own[c + 1 : c + 2])
        one = square(c, own[c], x_c, z_c, low)
        sq.append(one[0])
        low.append(one[1])
    keep, give, near = [], [], []
    for c in chunks:
        x_c = send(low[c], flip_x)
        u = send(low[c], flip_core)
        (acc,) = call(
            cube_own, [lists, low[c], u, after(band, low[-1], *near)], [acc_shapes[c]], dense[c]
        )
        x2.append(x_c)
        z2.append(send(x_c, move_z))
        cx = send(x_c, flip_core)
        (acc,) = call(cube_near, [lists, acc, x_c, cx, band], [acc_shapes[c]], dense[c], aliases={1: 0})
        near.append(acc)
    for c in chunks:
        z_c = after(z2[c], near[c], *give)
        one = call(
            cube_far,
            [lists, near[c], z_c, send(z_c, flip_core), band, sq[c]],
            [acc_shapes[c], shape((rb, slots, sizes[c], bs), f32), shape((n - 1, rb, slots, sizes[c], bs), bf16)],
            dense[c],
            aliases={1: 0},
        )[1:]
        keep.append(one[0])
        give.append(one[1])
    taken = [exchange(v) for v in give]

    def join(*refs):
        keep_refs, taken_refs, (out_ref, turned, done, sems) = refs[:cuts], refs[cuts : 2 * cuts], refs[-4:]
        q = lax.axis_index("inner")
        copies = [pltpu.make_async_copy(done.at[i], out_ref.at[i], sems.at[i]) for i in range(rb)]
        for i in range(rb):
            for s in range(slots):
                for c in chunks:
                    turned[i, s, piece(q, c), :] = keep_refs[c][i, s]
                    for m in range(1, n):
                        at = piece(lax.rem(q - m + n, n), c)
                        turned[i, s, at, :] = taken_refs[c][m - 1, i, s].astype(f32)
                done[i, s] = turned[i, s].T
            copies[i].start()
        for copy in copies:
            copy.wait()

    whole = pltpu.VMEM((rb, slots, bs, bs), f32)
    (out,) = call(
        join,
        [*keep, *taken],
        [shape((rb, slots, bs, bs), f32)],
        [whole, whole, pltpu.SemaphoreType.DMA((rb,))],
        hbm_out=True,
    )
    return out


def solution(mesh):
    in_specs = (P("rows", "inner", None, None), P(), P())
    out_specs = P("rows", "inner", None, None)
    return jax.shard_map(
        per_device, mesh=mesh, in_specs=in_specs, out_specs=out_specs, check_vma=False
    )
```

```python
import jax
import jax.numpy as jnp
from jax import lax
from jax.experimental import pallas as pl
from jax.experimental.pallas import tpu as pltpu
from jax.sharding import PartitionSpec as P

REACH = 2
BAND = 2 * REACH + 1
WIDE = 4 * REACH + 1
VMEM = pl.BlockSpec(memory_space=pltpu.VMEM)
HBM = pl.BlockSpec(memory_space=pltpu.HBM)
SMEM = pl.BlockSpec(memory_space=pltpu.SMEM)
PARAMS = pltpu.CompilerParams(vmem_limit_bytes=16 * 1024 * 1024)


def call(kernel, ins, outs, scratch=(), aliases=None, hbm_in=False, hbm_out=False, us=0):
    here = HBM if hbm_in else VMEM
    specs = [SMEM if x.dtype == jnp.int32 else here for x in ins]
    if not hbm_out:
        outs = [pltpu.VMEM(x.shape, x.dtype) for x in outs]
    place = pltpu.HBM if hbm_in else pltpu.VMEM
    ins = [
        x if x.dtype == jnp.int32 else pltpu.with_memory_space_constraint(x, place) for x in ins
    ]
    return pl.pallas_call(
        kernel,
        out_shape=tuple(outs),
        in_specs=specs,
        out_specs=tuple(HBM if hbm_out else VMEM for _ in outs),
        scratch_shapes=list(scratch),
        input_output_aliases=aliases or {},
        compiler_params=PARAMS,
        cost_estimate=us and pl.CostEstimate(flops=int(us * 1.1e9), transcendentals=0, bytes_accessed=1024) or None,
    )(*ins)


def after(x, *others):
    return lax.optimization_barrier((x, *others))[0]


def offsets(j):
    first = j < 2
    return {
        "own": 0,
        "x": jnp.where(first, 2, -2),
        "core": jnp.where(j % 2 == 0, 1, -1),
        "core_x": jnp.where(first, 1, -1),
        "z": jnp.where(first, -2, 2),
        "core_z": jnp.where(first, -1, 1),
    }


def per_device(p_blocks, col_lists, fill_lists):
    rb, slots, bs, _ = p_blocks.shape
    nb = col_lists.shape[0]
    fill = fill_lists.shape[1]
    n_rows = lax.axis_size("rows")
    n = lax.axis_size("inner")
    part = bs // n
    sizes = [part // 2] * 2 if part % 32 == 0 else [part]
    cuts = len(sizes)
    offs = [sum(sizes[:c]) for c in range(cuts)]
    unit = min(sizes)
    width = rb * bs
    bf16, f32 = jnp.bfloat16, jnp.float32
    shape = jax.ShapeDtypeStruct
    chunks = range(cuts)

    def shift(m):
        return [(i, (i + m) % n) for i in range(n)]

    def along(r):
        group, j = divmod(r, 4)
        return (group + (1 if j < 2 else -1)) % (n_rows // 4) * 4 + j

    flip_x = [(r, r ^ 2) for r in range(n_rows)]
    flip_core = [(r, r ^ 1) for r in range(n_rows)]
    move_z = [(r, along(r)) for r in range(n_rows)]

    def send(x, pairs, axis="rows"):
        return lax.ppermute(x, axis, pairs)

    def rows_at(index, size):
        return pl.ds(pl.multiple_of(index * size, size), size)

    def piece(index, c):
        return pl.ds(pl.multiple_of(index * part + offs[c], unit), sizes[c])

    def wrapped(x):
        return jnp.where(x < 0, x + nb, jnp.where(x >= nb, x - nb, x))

    def received(parts):
        return parts[0][None] if n == 2 else jnp.stack(parts)

    def nth(x, m):
        return x.reshape(x.shape[1:]) if n == 2 else x[m]

    def exchange(x):
        return received([send(nth(x, m - 1), shift(m), "inner") for m in range(1, n)])

    def pack(p_ref, mine_ref, *refs):
        rest_refs, (raw, turned, sems) = refs[:cuts], refs[-3:]
        q = lax.axis_index("inner")
        copies = [pltpu.make_async_copy(p_ref.at[i], raw.at[i], sems.at[i]) for i in range(rb)]
        for copy in copies:
            copy.start()
        for i in range(rb):
            copies[i].wait()
            for s in range(slots):
                turned[i, s] = raw[i, s].T
                mine_ref[i, s] = turned[i, s, rows_at(q, part), :]
                for c in chunks:
                    for m in range(1, n):
                        rest_refs[c][m - 1, i, s] = turned[i, s, piece(lax.rem(q + m, n), c), :]

    whole = pltpu.VMEM((rb, slots, bs, bs), bf16)
    packed = call(
        pack,
        [p_blocks],
        [shape((rb, slots, part, bs), bf16)]
        + [shape((n - 1, rb, slots, k, bs), bf16) for k in sizes],
        [whole, whole, pltpu.SemaphoreType.DMA((rb,))],
        hbm_in=True,
    )
    mine, rest = packed[0], packed[1:]
    lists = jnp.concatenate([col_lists.T, fill_lists.T], axis=1)

    def add(ref, where, lanes, value):
        ref[where, lanes] = (ref[where, lanes].astype(f32) + value.astype(f32)).astype(bf16)

    def column(lists_ref, i, slot):
        o = lax.axis_index("rows")
        return wrapped(lists_ref[slot, o * rb + i] - rb * (o - REACH))

    def start_rows(lists_ref, mine_ref, *refs):
        out_refs = refs[:cuts]
        q = lax.axis_index("inner")
        for c in chunks:
            out_refs[c][...] = jnp.zeros(out_refs[c].shape, bf16)
        for s in range(slots):
            for i in range(rb):
                at = column(lists_ref, i, q * slots + s)
                for c in chunks:
                    value = mine_ref[i, s, pl.ds(offs[c], sizes[c]), :]
                    add(out_refs[c], rows_at(at, sizes[c]), pl.ds(i * bs, bs), value)

    def start_band(lists_ref, *refs):
        rest_refs, out_ref = refs[:cuts], refs[-1]
        q = lax.axis_index("inner")
        out_ref[...] = jnp.zeros(out_ref.shape, bf16)
        for s in range(slots):
            for i in range(rb):
                at = column(lists_ref, i, q * slots + s) * n + lax.rem(q + 1, n)
                for c in chunks:
                    value = rest_refs[c][0, i, s]
                    add(out_ref, piece(at, c), pl.ds(i * bs, bs), value)

    def end_rows(lists_ref, in_ref, got_ref, out_ref):
        q = lax.axis_index("inner")
        for s in range(slots):
            for i in range(rb):
                for m in range(1, n):
                    at = column(lists_ref, i, lax.rem(q - m + n, n) * slots + s)
                    add(out_ref, rows_at(at, got_ref.shape[3]), pl.ds(i * bs, bs), got_ref[m - 1, i, s])

    def end_band(lists_ref, in_ref, left_ref, *refs):
        dense_refs, out_ref = refs[:cuts], refs[-1]
        q = lax.axis_index("inner")
        other = lax.rem(q + 1, n)
        for s in range(slots):
            for i in range(rb):
                at = column(lists_ref, i, other * slots + s) * n + other
                add(out_ref, rows_at(at, part), pl.ds(i * bs, bs), left_ref[i, s])
        for k in range(BAND * rb):
            for c in chunks:
                out_ref[piece(k * n + q, c), :] = dense_refs[c][pl.ds(k * sizes[c], sizes[c]), :]

    def whole_band(lists_ref, left_ref, out_ref):
        out_ref[...] = jnp.zeros(out_ref.shape, bf16)
        for g in range(n):
            for s in range(slots):
                for i in range(rb):
                    at = column(lists_ref, i, g * slots + s)
                    add(out_ref, rows_at(at, bs), pl.ds(i * bs, bs), left_ref[g, i, s].T)

    band_shape = shape((BAND * width, width), bf16)
    rows_shapes = [shape((BAND * rb * k, width), bf16) for k in sizes]
    acc_shapes = [shape((WIDE * rb * k, width), f32) for k in sizes]
    own = call(start_rows, [lists, mine], rows_shapes)
    got = [exchange(x) for x in rest]
    if n == 2:
        (band,) = call(start_band, [lists, *rest], [band_shape])
        left = send(after(mine, got[0]), shift(1), "inner")
    else:
        left = lax.all_gather(p_blocks, "inner", axis=0)
    own = [
        call(end_rows, [lists, own[c], got[c]], [rows_shapes[c]], aliases={1: 0}, us=20 * c)[0]
        for c in chunks
    ]
    if n == 2:
        (band,) = call(end_band, [lists, band, left, *own], [band_shape], aliases={1: 0}, us=20)
    else:
        (band,) = call(whole_band, [lists, left], [band_shape])

    def weights(left_ref, d):
        return left_ref[rows_at(d + REACH, width), :]

    def square_term(d, rows_ref, left_ref, acc_ref):
        term = jnp.dot(rows_ref[...], weights(left_ref, d), preferred_element_type=f32)
        span = rows_ref.shape[0]
        step = span // BAND
        acc_ref[pl.ds(pl.multiple_of((d + REACH) * step, step), span), :] += term

    def square_near(w, u, x, cx, left_ref, acc_ref):
        j = lax.rem(lax.axis_index("rows"), 4)
        d = offsets(j)
        span = w.shape[0]
        edge = span // BAND * REACH
        acc_ref[:edge, :] = jnp.zeros((edge, width), f32)
        acc_ref[edge : edge + span, :] = jnp.dot(
            w[...], left_ref[REACH * width : (REACH + 1) * width, :], preferred_element_type=f32
        )
        acc_ref[edge + span :, :] = jnp.zeros((edge, width), f32)
        square_term(d["core"], u, left_ref, acc_ref)
        square_term(d["x"], x, left_ref, acc_ref)

        @pl.when((j == 1) | (j == 2))
        def _():
            square_term(d["core_x"], cx, left_ref, acc_ref)

    def square_far(lists_ref, acc_in, z, cz, left_ref, acc_ref, sq_ref, low_ref):
        j = lax.rem(lax.axis_index("rows"), 4)
        d = offsets(j)
        square_term(d["z"], z, left_ref, acc_ref)

        @pl.when((j == 0) | (j == 3))
        def _():
            square_term(d["core_z"], cz, left_ref, acc_ref)

        for v in range(fill):
            for i in range(rb):
                value = acc_ref[kept(lists_ref, i, v, sq_ref.shape[2]), pl.ds(i * bs, bs)]
                sq_ref[i, v] = value
                low_ref[i, v] = value.astype(bf16)

    def kept(lists_ref, i, v, cols):
        o = lax.axis_index("rows")
        return rows_at(wrapped(lists_ref[v, nb + o * rb + i] - rb * (o - 2 * REACH)), cols)

    def cube_term(lists_ref, d, reach, low_ref, left_ref, dense, acc_ref, first=False):
        o = lax.axis_index("rows")
        source = lax.rem(o + d + n_rows, n_rows)
        blocks = (WIDE - reach) * rb
        cols = low_ref.shape[2]
        start = jnp.maximum(d, 0) * rb
        rows = blocks * cols
        dense[:rows, :] = jnp.zeros((rows, width), bf16)
        for v in range(fill):
            for k in range(rb):
                c = wrapped(lists_ref[v, nb + source * rb + k] - rb * (o - 2 * REACH)) - start
                c = jnp.where((c >= 0) & (c < blocks), c, blocks)
                dense[rows_at(c, cols), pl.ds(k * bs, bs)] = low_ref[k, v]

        term = jnp.dot(dense[:rows, :], weights(left_ref, d), preferred_element_type=f32)
        if first:
            acc_ref[...] = term
        else:
            acc_ref[pl.ds(pl.multiple_of(start * cols, rb * cols), rows), :] += term

    def cube_own(lists_ref, w, u, left_ref, acc_ref, dense):
        d = offsets(lax.rem(lax.axis_index("rows"), 4))
        cube_term(lists_ref, 0, 0, w, left_ref, dense, acc_ref, first=True)
        cube_term(lists_ref, d["core"], 1, u, left_ref, dense, acc_ref)

    def cube_near(lists_ref, acc_in, x, cx, left_ref, acc_ref, dense):
        j = lax.rem(lax.axis_index("rows"), 4)
        d = offsets(j)
        cube_term(lists_ref, d["x"], 2, x, left_ref, dense, acc_ref)

        @pl.when((j == 1) | (j == 2))
        def _():
            cube_term(lists_ref, d["core_x"], 1, cx, left_ref, dense, acc_ref)

    def cube_far(lists_ref, acc_in, z, cz, left_ref, sq_ref, acc_ref, keep_ref, give_ref, dense):
        q = lax.axis_index("inner")
        j = lax.rem(lax.axis_index("rows"), 4)
        d = offsets(j)
        cube_term(lists_ref, d["z"], 2, z, left_ref, dense, acc_ref)

        @pl.when((j == 0) | (j == 3))
        def _():
            cube_term(lists_ref, d["core_z"], 1, cz, left_ref, dense, acc_ref)

        def result(i, v):
            return 3.0 * sq_ref[i, v] - 2.0 * acc_ref[kept(lists_ref, i, v, sq_ref.shape[2]), pl.ds(i * bs, bs)]

        for s in range(slots):
            for i in range(rb):
                keep_ref[i, s] = result(i, q * slots + s)
                for m in range(1, n):
                    give_ref[m - 1, i, s] = result(i, lax.rem(q + m, n) * slots + s).astype(bf16)

    dense = [[pltpu.VMEM(((WIDE * rb + 1) * k, width), bf16)] for k in sizes]
    x, z, sq, low, x2, z2 = [], [], [], [], [], []
    close = []
    for c in chunks:
        u = send(own[c], flip_core)
        x_c = after(send(own[c], flip_x), *own[c + 1 : c + 2], *close)
        z.append(send(x_c, move_z))
        cx = send(x_c, flip_core)
        close += call(square_near, [own[c], u, x_c, cx, band], [acc_shapes[c]], us=20 * c or 20)
        x.append(x_c)
    for c in chunks:
        z_c = after(z[c], close[c], *x[c + 1 : c + 2])
        cz = after(send(z_c, flip_core), *close[c + 1 : c + 2])
        kept_shape = (rb, fill, sizes[c], bs)
        one = call(
            square_far,
            [lists, close[c], z_c, cz, band],
            [acc_shapes[c], shape(kept_shape, f32), shape(kept_shape, bf16)],
            aliases={1: 0},
        )
        sq.append(one[1])
        low.append(one[2])
    keep, give, near = [], [], []
    for c in chunks:
        x_c = send(low[c], flip_x)
        u = send(low[c], flip_core)
        (acc,) = call(
            cube_own, [lists, low[c], u, after(band, low[-1], *near)], [acc_shapes[c]], dense[c], us=20 * c
        )
        x2.append(x_c)
        z2.append(send(x_c, move_z))
        cx = send(x_c, flip_core)
        (acc,) = call(cube_near, [lists, acc, x_c, cx, band], [acc_shapes[c]], dense[c], aliases={1: 0}, us=20 * c)
        near.append(acc)
    for c in chunks:
        z_c = after(z2[c], near[c], *give)
        one = call(
            cube_far,
            [lists, near[c], z_c, send(z_c, flip_core), band, sq[c]],
            [acc_shapes[c], shape((rb, slots, sizes[c], bs), f32), shape((n - 1, rb, slots, sizes[c], bs), bf16)],
            dense[c],
            aliases={1: 0},
        )[1:]
        keep.append(one[0])
        give.append(one[1])
    taken = [exchange(v) for v in give]

    def join(*refs):
        keep_refs, taken_refs, (out_ref, turned, done, sems) = refs[:cuts], refs[cuts : 2 * cuts], refs[-4:]
        q = lax.axis_index("inner")
        copies = [pltpu.make_async_copy(done.at[i], out_ref.at[i], sems.at[i]) for i in range(rb)]
        for i in range(rb):
            for s in range(slots):
                for c in chunks:
                    turned[i, s, piece(q, c), :] = keep_refs[c][i, s]
                    for m in range(1, n):
                        at = piece(lax.rem(q - m + n, n), c)
                        turned[i, s, at, :] = taken_refs[c][m - 1, i, s].astype(f32)
                done[i, s] = turned[i, s].T
            copies[i].start()
        for copy in copies:
            copy.wait()

    whole = pltpu.VMEM((rb, slots, bs, bs), f32)
    (out,) = call(
        join,
        [*keep, *taken],
        [shape((rb, slots, bs, bs), f32)],
        [whole, whole, pltpu.SemaphoreType.DMA((rb,))],
        hbm_out=True,
    )
    return out


def solution(mesh):
    in_specs = (P("rows", "inner", None, None), P(), P())
    out_specs = P("rows", "inner", None, None)
    return jax.shard_map(
        per_device, mesh=mesh, in_specs=in_specs, out_specs=out_specs, check_vma=False
    )
```

```python
import jax
import jax.numpy as jnp
from jax import lax
from jax.experimental import pallas as pl
from jax.experimental.pallas import tpu as pltpu
from jax.sharding import PartitionSpec as P

REACH = 2
BAND = 2 * REACH + 1
WIDE = 4 * REACH + 1
VMEM = pl.BlockSpec(memory_space=pltpu.VMEM)
HBM = pl.BlockSpec(memory_space=pltpu.HBM)
SMEM = pl.BlockSpec(memory_space=pltpu.SMEM)
PARAMS = pltpu.CompilerParams(vmem_limit_bytes=16 * 1024 * 1024)


def call(kernel, ins, outs, scratch=(), aliases=None, hbm_in=(), hbm_out=False, us=0):
    specs = [SMEM if x.dtype == jnp.int32 else HBM if a in hbm_in else VMEM for a, x in enumerate(ins)]
    if not hbm_out:
        outs = [(pltpu.SMEM if x.dtype == jnp.int32 else pltpu.VMEM)(x.shape, x.dtype) for x in outs]
    ins = [
        pltpu.with_memory_space_constraint(
            x, pltpu.SMEM if x.dtype == jnp.int32 else pltpu.HBM if a in hbm_in else pltpu.VMEM
        )
        for a, x in enumerate(ins)
    ]
    return pl.pallas_call(
        kernel,
        out_shape=tuple(outs),
        in_specs=specs,
        out_specs=tuple(SMEM if x.dtype == jnp.int32 else HBM if hbm_out else VMEM for x in outs),
        scratch_shapes=list(scratch),
        input_output_aliases=aliases or {},
        compiler_params=PARAMS,
        cost_estimate=us and pl.CostEstimate(flops=int(us * 1.1e9), transcendentals=0, bytes_accessed=1024) or None,
    )(*ins)


def after(x, *others):
    return lax.optimization_barrier((x, *others))[0]


def offsets(j):
    first = j < 2
    return {
        "own": 0,
        "x": jnp.where(first, 2, -2),
        "core": jnp.where(j % 2 == 0, 1, -1),
        "core_x": jnp.where(first, 1, -1),
        "z": jnp.where(first, -2, 2),
        "core_z": jnp.where(first, -1, 1),
    }


def per_device(p_blocks, col_lists, fill_lists):
    rb, slots, bs, _ = p_blocks.shape
    nb = col_lists.shape[0]
    fill = fill_lists.shape[1]
    n_rows = lax.axis_size("rows")
    n = lax.axis_size("inner")
    part = bs // n
    sizes = [part // 2] * 2 if part % 32 == 0 else [part]
    cuts = len(sizes)
    offs = [sum(sizes[:c]) for c in range(cuts)]
    unit = min(sizes)
    width = rb * bs
    bf16, f32 = jnp.bfloat16, jnp.float32
    shape = jax.ShapeDtypeStruct
    chunks = range(cuts)

    def shift(m):
        return [(i, (i + m) % n) for i in range(n)]

    def along(r):
        group, j = divmod(r, 4)
        return (group + (1 if j < 2 else -1)) % (n_rows // 4) * 4 + j

    flip_x = [(r, r ^ 2) for r in range(n_rows)]
    flip_core = [(r, r ^ 1) for r in range(n_rows)]
    move_z = [(r, along(r)) for r in range(n_rows)]

    def send(x, pairs, axis="rows"):
        return lax.ppermute(x, axis, pairs)

    def rows_at(index, size):
        return pl.ds(pl.multiple_of(index * size, size), size)

    def piece(index, c):
        return pl.ds(pl.multiple_of(index * part + offs[c], unit), sizes[c])

    def wrapped(x):
        return jnp.where(x < 0, x + nb, jnp.where(x >= nb, x - nb, x))

    def received(parts):
        return parts[0][None] if n == 2 else jnp.stack(parts)

    def nth(x, m):
        return x.reshape(x.shape[1:]) if n == 2 else x[m]

    def exchange(x):
        return received([send(nth(x, m - 1), shift(m), "inner") for m in range(1, n)])

    def pack(p_ref, mine_ref, *refs):
        rest_refs, (raw, turned, sems) = refs[:cuts], refs[-3:]
        q = lax.axis_index("inner")
        copies = [pltpu.make_async_copy(p_ref.at[i], raw.at[i], sems.at[i]) for i in range(rb)]
        for copy in copies:
            copy.start()
        for i in range(rb):
            copies[i].wait()
            for s in range(slots):
                turned[i, s] = raw[i, s].T
                mine_ref[i, s] = turned[i, s, rows_at(q, part), :]
                for c in chunks:
                    for m in range(1, n):
                        rest_refs[c][m - 1, i, s] = turned[i, s, piece(lax.rem(q + m, n), c), :]

    whole = pltpu.VMEM((rb, slots, bs, bs), bf16)
    packed = call(
        pack,
        [p_blocks],
        [shape((rb, slots, part, bs), bf16)]
        + [shape((n - 1, rb, slots, k, bs), bf16) for k in sizes],
        [whole, whole, pltpu.SemaphoreType.DMA((rb,))],
        hbm_in=(0,),
    )
    mine, rest = packed[0], packed[1:]
    lists = jnp.concatenate([col_lists.T, fill_lists.T], axis=1)

    def keep_lists(in_ref, out_ref, sem):
        copy = pltpu.make_async_copy(in_ref, out_ref, sem)
        copy.start()
        copy.wait()

    (lists,) = pl.pallas_call(
        keep_lists,
        out_shape=(pltpu.SMEM(lists.shape, lists.dtype),),
        in_specs=[VMEM],
        out_specs=(SMEM,),
        scratch_shapes=[pltpu.SemaphoreType.DMA],
        compiler_params=PARAMS,
    )(lists)

    def add(ref, where, lanes, value):
        ref[where, lanes] = (ref[where, lanes].astype(f32) + value.astype(f32)).astype(bf16)

    def add_apart(terms):
        sums = [(ref[at].astype(f32) + value.astype(f32)).astype(bf16) for ref, at, value in terms]
        for (ref, at, _), value in zip(terms, sums):
            ref[at] = value

    def column(lists_ref, i, slot):
        o = lax.axis_index("rows")
        return wrapped(lists_ref[slot, o * rb + i] - rb * (o - REACH))

    def start_rows(lists_ref, mine_ref, *refs):
        out_refs = refs[:cuts]
        q = lax.axis_index("inner")
        for c in chunks:
            out_refs[c][...] = jnp.zeros(out_refs[c].shape, bf16)
        for s in range(slots):
            terms = []
            for i in range(rb):
                at = column(lists_ref, i, q * slots + s)
                for c in chunks:
                    value = mine_ref[i, s, pl.ds(offs[c], sizes[c]), :]
                    terms.append((out_refs[c], (rows_at(at, sizes[c]), pl.ds(i * bs, bs)), value))
            add_apart(terms)

    def start_band(lists_ref, *refs):
        rest_refs, out_ref = refs[:cuts], refs[-1]
        q = lax.axis_index("inner")
        out_ref[...] = jnp.zeros(out_ref.shape, bf16)
        for s in range(slots):
            terms = []
            for i in range(rb):
                at = column(lists_ref, i, q * slots + s) * n + lax.rem(q + 1, n)
                for c in chunks:
                    terms.append((out_ref, (piece(at, c), pl.ds(i * bs, bs)), rest_refs[c][0, i, s]))
            add_apart(terms)

    def end_rows(lists_ref, in_ref, got_ref, out_ref):
        q = lax.axis_index("inner")
        for s in range(slots):
            for m in range(1, n):
                terms = []
                for i in range(rb):
                    at = column(lists_ref, i, lax.rem(q - m + n, n) * slots + s)
                    place = rows_at(at, got_ref.shape[3]), pl.ds(i * bs, bs)
                    terms.append((out_ref, place, got_ref[m - 1, i, s]))
                add_apart(terms)

    def end_band(lists_ref, in_ref, left_ref, *refs):
        dense_refs, out_ref = refs[:cuts], refs[-1]
        q = lax.axis_index("inner")
        other = lax.rem(q + 1, n)
        for s in range(slots):
            terms = []
            for i in range(rb):
                at = column(lists_ref, i, other * slots + s) * n + other
                terms.append((out_ref, (rows_at(at, part), pl.ds(i * bs, bs)), left_ref[i, s]))
            add_apart(terms)
        for k in range(BAND * rb):
            for c in chunks:
                out_ref[piece(k * n + q, c), :] = dense_refs[c][pl.ds(k * sizes[c], sizes[c]), :]

    def whole_band(lists_ref, left_ref, out_ref):
        out_ref[...] = jnp.zeros(out_ref.shape, bf16)
        for g in range(n):
            for s in range(slots):
                for i in range(rb):
                    at = column(lists_ref, i, g * slots + s)
                    add(out_ref, rows_at(at, bs), pl.ds(i * bs, bs), left_ref[g, i, s].T)

    band_shape = shape((BAND * width, width), bf16)
    rows_shapes = [shape((BAND * rb * k, width), bf16) for k in sizes]
    acc_shapes = [shape((WIDE * rb * k, width), f32) for k in sizes]
    own = call(start_rows, [lists, mine], rows_shapes)
    if n == 2:
        (band,) = call(start_band, [lists, *rest], [band_shape])
        rest = [rest[0], *(after(x, band) for x in rest[1:])]
    got = [exchange(x) for x in rest]
    if n == 2:
        left = send(after(mine, got[0]), shift(1), "inner")
    else:
        left = lax.all_gather(p_blocks, "inner", axis=0)
    own = [
        call(end_rows, [lists, own[c], got[c]], [rows_shapes[c]], aliases={1: 0}, us=20 * c)[0]
        for c in chunks
    ]
    if n == 2:
        (band,) = call(end_band, [lists, band, left, *own], [band_shape], aliases={1: 0}, us=20)
    else:
        (band,) = call(whole_band, [lists, left], [band_shape])

    def weights(left_ref, d):
        return left_ref[rows_at(d + REACH, width), :]

    def square_term(d, rows_ref, left_ref, acc_ref):
        term = jnp.dot(rows_ref[...], weights(left_ref, d), preferred_element_type=f32)
        span = rows_ref.shape[0]
        step = span // BAND
        acc_ref[pl.ds(pl.multiple_of((d + REACH) * step, step), span), :] += term

    def square_near(w, u, x, cx, left_ref, acc_ref):
        j = lax.rem(lax.axis_index("rows"), 4)
        d = offsets(j)
        span = w.shape[0]
        edge = span // BAND * REACH
        acc_ref[:edge, :] = jnp.zeros((edge, width), f32)
        acc_ref[edge : edge + span, :] = jnp.dot(
            w[...], left_ref[REACH * width : (REACH + 1) * width, :], preferred_element_type=f32
        )
        acc_ref[edge + span :, :] = jnp.zeros((edge, width), f32)
        square_term(d["core"], u, left_ref, acc_ref)
        square_term(d["x"], x, left_ref, acc_ref)

        @pl.when((j == 1) | (j == 2))
        def _():
            square_term(d["core_x"], cx, left_ref, acc_ref)

    def square_z(acc_in, z, left_ref, acc_ref):
        square_term(offsets(lax.rem(lax.axis_index("rows"), 4))["z"], z, left_ref, acc_ref)

    def square_far(lists_ref, acc_in, cz, left_ref, acc_ref, low_ref):
        j = lax.rem(lax.axis_index("rows"), 4)

        @pl.when((j == 0) | (j == 3))
        def _():
            square_term(offsets(j)["core_z"], cz, left_ref, acc_ref)

        for v in range(fill):
            for i in range(rb):
                where = kept(lists_ref, i, v, low_ref.shape[2])
                low_ref[i, v] = acc_ref[where, pl.ds(i * bs, bs)].astype(bf16)

    def kept(lists_ref, i, v, cols):
        o = lax.axis_index("rows")
        return rows_at(wrapped(lists_ref[v, nb + o * rb + i] - rb * (o - 2 * REACH)), cols)

    def window(d, reach):
        return (WIDE - reach) * rb, jnp.maximum(d, 0) * rb

    def spread(lists_ref, d, reach, low_ref, dense):
        o = lax.axis_index("rows")
        source = lax.rem(o + d + n_rows, n_rows)
        blocks, start = window(d, reach)
        cols = low_ref.shape[2]
        dense[: blocks * cols, :] = jnp.zeros((blocks * cols, width), bf16)
        for v in range(fill):
            for k in range(rb):
                c = wrapped(lists_ref[v, nb + source * rb + k] - rb * (o - 2 * REACH)) - start
                c = jnp.where((c >= 0) & (c < blocks), c, blocks)
                dense[rows_at(c, cols), pl.ds(k * bs, bs)] = low_ref[k, v]

    def multiply(d, reach, dense, left_ref, acc_ref, first=0, end=rb, fresh=False):
        blocks, start = window(d, reach)
        cols = dense.shape[0] // (WIDE * rb + 1)
        rows, lanes = blocks * cols, pl.ds(first * bs, (end - first) * bs)
        term = jnp.dot(
            dense[:rows, :], left_ref[rows_at(d + REACH, width), lanes], preferred_element_type=f32
        )
        if fresh:
            acc_ref[...] = term
        else:
            acc_ref[pl.ds(pl.multiple_of(start * cols, rb * cols), rows), lanes] += term

    def cube_term(lists_ref, d, reach, low_ref, left_ref, dense, acc_ref, first=False):
        spread(lists_ref, d, reach, low_ref, dense)
        multiply(d, reach, dense, left_ref, acc_ref, fresh=first)

    def cube_own(lists_ref, w, u, left_ref, acc_ref, dense):
        d = offsets(lax.rem(lax.axis_index("rows"), 4))
        cube_term(lists_ref, 0, 0, w, left_ref, dense, acc_ref, first=True)
        cube_term(lists_ref, d["core"], 1, u, left_ref, dense, acc_ref)

    def cube_near(lists_ref, acc_in, x, cx, left_ref, acc_ref, dense):
        j = lax.rem(lax.axis_index("rows"), 4)
        d = offsets(j)
        cube_term(lists_ref, d["x"], 2, x, left_ref, dense, acc_ref)

        @pl.when((j == 1) | (j == 2))
        def _():
            cube_term(lists_ref, d["core_x"], 1, cx, left_ref, dense, acc_ref)

    def cube_far(lists_ref, acc_in, z, cz, left_ref, square_ref, acc_ref, keep_ref, give_ref, dense):
        j = lax.rem(lax.axis_index("rows"), 4)
        d = offsets(j)
        cube_term(lists_ref, d["z"], 2, z, left_ref, dense, acc_ref)

        @pl.when((j == 0) | (j == 3))
        def _():
            cube_term(lists_ref, d["core_z"], 1, cz, left_ref, dense, acc_ref)

        results(0, rb, lists_ref, square_ref, acc_ref, keep_ref, give_ref)

    def results(first, end, lists_ref, square_ref, acc_ref, keep_ref, give_ref):
        q = lax.axis_index("inner")

        def result(i, v):
            at = kept(lists_ref, i, v, keep_ref.shape[2]), pl.ds(i * bs, bs)
            return 3.0 * square_ref[at] - 2.0 * acc_ref[at]

        for s in range(slots):
            for i in range(first, end):
                keep_ref[i - first, s] = result(i, q * slots + s)
                for m in range(1, n):
                    v = lax.rem(q + m, n) * slots + s
                    give_ref[m - 1, i - first, s] = result(i, v).astype(bf16)

    def cube_last(lists_ref, acc_in, z, cz, left_ref, square_ref, acc_ref, dense_z, dense_cz, keep_ref, give_ref):
        j = lax.rem(lax.axis_index("rows"), 4)
        d = offsets(j)
        spread(lists_ref, d["z"], 2, z, dense_z)
        multiply(d["z"], 2, dense_z, left_ref, acc_ref, 0, early)

        @pl.when((j == 0) | (j == 3))
        def _():
            spread(lists_ref, d["core_z"], 1, cz, dense_cz)
            multiply(d["core_z"], 1, dense_cz, left_ref, acc_ref, 0, early)

        results(0, early, lists_ref, square_ref, acc_ref, keep_ref, give_ref)

    def cube_end(lists_ref, acc_in, dense_z, dense_cz, left_ref, square_ref, acc_ref, keep_ref, give_ref):
        j = lax.rem(lax.axis_index("rows"), 4)
        d = offsets(j)
        multiply(d["z"], 2, dense_z, left_ref, acc_ref, early)

        @pl.when((j == 0) | (j == 3))
        def _():
            multiply(d["core_z"], 1, dense_cz, left_ref, acc_ref, early)

        results(early, rb, lists_ref, square_ref, acc_ref, keep_ref, give_ref)

    dense = [[pltpu.VMEM(((WIDE * rb + 1) * k, width), bf16)] for k in sizes]
    x, z, sq, low, x2, z2 = [], [], [], [], [], []
    close = []
    for c in chunks:
        u = send(own[c], flip_core)
        x_c = after(send(own[c], flip_x), *own[c + 1 : c + 2], *close)
        z.append(send(x_c, move_z))
        cx = send(x_c, flip_core)
        close += call(square_near, [own[c], u, x_c, cx, band], [acc_shapes[c]], us=20 * c or 20)
        x.append(x_c)
    for c in chunks:
        z_c = after(z[c], close[c], *x[c + 1 : c + 2])
        cz = after(send(z_c, flip_core), *close[c + 1 : c + 2])
        (acc,) = call(square_z, [close[c], z_c, band], [acc_shapes[c]], aliases={0: 0})
        one = call(
            square_far,
            [lists, acc, cz, band],
            [acc_shapes[c], shape((rb, fill, sizes[c], bs), bf16)],
            aliases={1: 0},
        )
        sq.append(one[0])
        low.append(one[1])
    keep, give, near = [], [], []
    for c in chunks:
        x_c = send(low[c], flip_x)
        u = send(low[c], flip_core)
        (acc,) = call(
            cube_own, [lists, low[c], u, after(band, low[-1], *near)], [acc_shapes[c]], dense[c], us=20 * c
        )
        x2.append(x_c)
        z2.append(send(x_c, move_z))
        cx = send(x_c, flip_core)
        (acc,) = call(cube_near, [lists, acc, x_c, cx, band], [acc_shapes[c]], dense[c], aliases={1: 0}, us=20 * c)
        near.append(acc)
    early = rb - rb // 3

    def result_shapes(c, count):
        kept_shape = (count, slots, sizes[c], bs)
        return [shape(kept_shape, f32), shape((n - 1, *kept_shape), bf16)]

    taken = []
    for c in chunks[:-1]:
        z_c = after(z2[c], near[c], *give)
        one = call(
            cube_far,
            [lists, near[c], z_c, send(z_c, flip_core), band, sq[c]],
            [acc_shapes[c], *result_shapes(c, rb)],
            dense[c],
            aliases={1: 0},
        )[1:]
        keep.append(one[0])
        give.append(one[1])
        taken.append(exchange(one[1]))
    c = cuts - 1
    z_c = after(z2[c], near[c], *give)
    dense_shape = shape(dense[c][0].shape, bf16)
    acc, dense_z, dense_cz, keep_a, give_a = call(
        cube_last,
        [lists, near[c], z_c, send(z_c, flip_core), band, sq[c]],
        [acc_shapes[c], dense_shape, dense_shape, *result_shapes(c, early)],
        aliases={1: 0},
    )
    taken_a = exchange(give_a)
    _, keep_b, give_b = call(
        cube_end,
        [lists, acc, dense_z, dense_cz, band, sq[c]],
        [acc_shapes[c], *result_shapes(c, rb - early)],
        aliases={1: 0},
    )
    taken_b = exchange(give_b)

    def join(first, end, keep_refs, taken_refs, out_ref, turned, done, sems):
        q = lax.axis_index("inner")
        copies = {i: pltpu.make_async_copy(done.at[i], out_ref.at[i], sems.at[i]) for i in range(first, end)}
        for i in range(first, end):
            for s in range(slots):
                for c in chunks:
                    k = i - first if c == cuts - 1 else i
                    turned[i, s, piece(q, c), :] = keep_refs[c][k, s]
                    for m in range(1, n):
                        at = piece(lax.rem(q - m + n, n), c)
                        turned[i, s, at, :] = taken_refs[c][m - 1, k, s].astype(f32)
                done[i, s] = turned[i, s].T
            copies[i].start()
        for copy in copies.values():
            copy.wait()

    def join_first(*refs):
        join(0, early, refs[:cuts], refs[cuts : 2 * cuts], *refs[2 * cuts :])

    def join_rest(*refs):
        join(early, rb, refs[:cuts], refs[cuts : 2 * cuts], *refs[2 * cuts + 1 :])

    whole = pltpu.VMEM((rb, slots, bs, bs), f32)
    scratch = [whole, whole, pltpu.SemaphoreType.DMA((rb,))]
    out_shape = [shape((rb, slots, bs, bs), f32)]
    (out,) = call(join_first, [*keep, keep_a, *taken, taken_a], out_shape, scratch, hbm_out=True)
    (out,) = call(
        join_rest,
        [*keep, keep_b, *taken, taken_b, out],
        out_shape,
        scratch,
        aliases={2 * cuts: 0},
        hbm_in=(2 * cuts,),
        hbm_out=True,
    )
    return out


def solution(mesh):
    in_specs = (P("rows", "inner", None, None), P(), P())
    out_specs = P("rows", "inner", None, None)
    return jax.shard_map(
        per_device, mesh=mesh, in_specs=in_specs, out_specs=out_specs, check_vma=False
    )
```

```python
import jax
import jax.numpy as jnp
from jax import lax
from jax.experimental import pallas as pl
from jax.experimental.pallas import tpu as pltpu
from jax.sharding import PartitionSpec as P

REACH = 2
BAND = 2 * REACH + 1
WIDE = 4 * REACH + 1
VMEM = pl.BlockSpec(memory_space=pltpu.VMEM)
HBM = pl.BlockSpec(memory_space=pltpu.HBM)
SMEM = pl.BlockSpec(memory_space=pltpu.SMEM)
PARAMS = pltpu.CompilerParams(vmem_limit_bytes=16 * 1024 * 1024)


def call(kernel, ins, outs, scratch=(), aliases=None, hbm_in=(), hbm_out=False, us=0):
    specs = [SMEM if x.dtype == jnp.int32 else HBM if a in hbm_in else VMEM for a, x in enumerate(ins)]
    if not hbm_out:
        outs = [(pltpu.SMEM if x.dtype == jnp.int32 else pltpu.VMEM)(x.shape, x.dtype) for x in outs]
    ins = [
        pltpu.with_memory_space_constraint(
            x, pltpu.SMEM if x.dtype == jnp.int32 else pltpu.HBM if a in hbm_in else pltpu.VMEM
        )
        for a, x in enumerate(ins)
    ]
    return pl.pallas_call(
        kernel,
        out_shape=tuple(outs),
        in_specs=specs,
        out_specs=tuple(SMEM if x.dtype == jnp.int32 else HBM if hbm_out else VMEM for x in outs),
        scratch_shapes=list(scratch),
        input_output_aliases=aliases or {},
        compiler_params=PARAMS,
        cost_estimate=us and pl.CostEstimate(flops=int(us * 1.1e9), transcendentals=0, bytes_accessed=1024) or None,
    )(*ins)


def after(x, *others):
    return lax.optimization_barrier((x, *others))[0]


def offsets(j):
    first = j < 2
    return {
        "own": 0,
        "x": jnp.where(first, 2, -2),
        "core": jnp.where(j % 2 == 0, 1, -1),
        "core_x": jnp.where(first, 1, -1),
        "z": jnp.where(first, -2, 2),
        "core_z": jnp.where(first, -1, 1),
    }


def per_device(p_blocks, col_lists, fill_lists):
    rb, slots, bs, _ = p_blocks.shape
    nb = col_lists.shape[0]
    fill = fill_lists.shape[1]
    n_rows = lax.axis_size("rows")
    n = lax.axis_size("inner")
    part = bs // n
    sizes = [part // 2] * 2 if part % 32 == 0 else [part]
    cuts = len(sizes)
    offs = [sum(sizes[:c]) for c in range(cuts)]
    unit = min(sizes)
    width = rb * bs
    bf16, f32 = jnp.bfloat16, jnp.float32
    shape = jax.ShapeDtypeStruct
    chunks = range(cuts)

    def shift(m):
        return [(i, (i + m) % n) for i in range(n)]

    def along(r):
        group, j = divmod(r, 4)
        return (group + (1 if j < 2 else -1)) % (n_rows // 4) * 4 + j

    flip_x = [(r, r ^ 2) for r in range(n_rows)]
    flip_core = [(r, r ^ 1) for r in range(n_rows)]
    move_z = [(r, along(r)) for r in range(n_rows)]

    def send(x, pairs, axis="rows"):
        return lax.ppermute(x, axis, pairs)

    def rows_at(index, size):
        return pl.ds(pl.multiple_of(index * size, size), size)

    def piece(index, c):
        return pl.ds(pl.multiple_of(index * part + offs[c], unit), sizes[c])

    def wrapped(x):
        return jnp.where(x < 0, x + nb, jnp.where(x >= nb, x - nb, x))

    def received(parts):
        return parts[0][None] if n == 2 else jnp.stack(parts)

    def nth(x, m):
        return x.reshape(x.shape[1:]) if n == 2 else x[m]

    def exchange(x):
        return received([send(nth(x, m - 1), shift(m), "inner") for m in range(1, n)])

    def pack(p_ref, mine_ref, *refs):
        rest_refs, (raw, turned, sems) = refs[:cuts], refs[-3:]
        q = lax.axis_index("inner")
        copies = [pltpu.make_async_copy(p_ref.at[i], raw.at[i], sems.at[i]) for i in range(rb)]
        for copy in copies:
            copy.start()
        for i in range(rb):
            copies[i].wait()
            for s in range(slots):
                turned[i, s] = raw[i, s].T
                mine_ref[i, s] = turned[i, s, rows_at(q, part), :]
                for c in chunks:
                    for m in range(1, n):
                        rest_refs[c][m - 1, i, s] = turned[i, s, piece(lax.rem(q + m, n), c), :]

    whole = pltpu.VMEM((rb, slots, bs, bs), bf16)
    packed = call(
        pack,
        [p_blocks],
        [shape((rb, slots, part, bs), bf16)]
        + [shape((n - 1, rb, slots, k, bs), bf16) for k in sizes],
        [whole, whole, pltpu.SemaphoreType.DMA((rb,))],
        hbm_in=(0,),
    )
    mine, rest = packed[0], packed[1:]
    lists = jnp.concatenate([col_lists.T, fill_lists.T], axis=1)

    def keep_lists(in_ref, out_ref, sem):
        copy = pltpu.make_async_copy(in_ref, out_ref, sem)
        copy.start()
        copy.wait()

    (lists,) = pl.pallas_call(
        keep_lists,
        out_shape=(pltpu.SMEM(lists.shape, lists.dtype),),
        in_specs=[VMEM],
        out_specs=(SMEM,),
        scratch_shapes=[pltpu.SemaphoreType.DMA],
        compiler_params=PARAMS,
    )(lists)

    def add(ref, where, lanes, value):
        ref[where, lanes] = (ref[where, lanes].astype(f32) + value.astype(f32)).astype(bf16)

    def add_apart(terms):
        sums = [(ref[at].astype(f32) + value.astype(f32)).astype(bf16) for ref, at, value in terms]
        for (ref, at, _), value in zip(terms, sums):
            ref[at] = value

    def column(lists_ref, i, slot):
        o = lax.axis_index("rows")
        return wrapped(lists_ref[slot, o * rb + i] - rb * (o - REACH))

    def start_rows(lists_ref, mine_ref, *refs):
        out_refs = refs[:cuts]
        q = lax.axis_index("inner")
        for c in chunks:
            out_refs[c][...] = jnp.zeros(out_refs[c].shape, bf16)
        for s in range(slots):
            terms = []
            for i in range(rb):
                at = column(lists_ref, i, q * slots + s)
                for c in chunks:
                    value = mine_ref[i, s, pl.ds(offs[c], sizes[c]), :]
                    terms.append((out_refs[c], (rows_at(at, sizes[c]), pl.ds(i * bs, bs)), value))
            add_apart(terms)

    def start_band(lists_ref, *refs):
        rest_refs, out_ref = refs[:cuts], refs[-1]
        q = lax.axis_index("inner")
        out_ref[...] = jnp.zeros(out_ref.shape, bf16)
        for s in range(slots):
            terms = []
            for i in range(rb):
                at = column(lists_ref, i, q * slots + s) * n + lax.rem(q + 1, n)
                for c in chunks:
                    terms.append((out_ref, (piece(at, c), pl.ds(i * bs, bs)), rest_refs[c][0, i, s]))
            add_apart(terms)

    def end_rows(lists_ref, in_ref, got_ref, out_ref):
        q = lax.axis_index("inner")
        for s in range(slots):
            for m in range(1, n):
                terms = []
                for i in range(rb):
                    at = column(lists_ref, i, lax.rem(q - m + n, n) * slots + s)
                    place = rows_at(at, got_ref.shape[3]), pl.ds(i * bs, bs)
                    terms.append((out_ref, place, got_ref[m - 1, i, s]))
                add_apart(terms)

    def end_band(lists_ref, in_ref, left_ref, *refs):
        dense_refs, out_ref = refs[:cuts], refs[-1]
        q = lax.axis_index("inner")
        other = lax.rem(q + 1, n)
        for s in range(slots):
            terms = []
            for i in range(rb):
                at = column(lists_ref, i, other * slots + s) * n + other
                terms.append((out_ref, (rows_at(at, part), pl.ds(i * bs, bs)), left_ref[i, s]))
            add_apart(terms)
        for k in range(BAND * rb):
            for c in chunks:
                out_ref[piece(k * n + q, c), :] = dense_refs[c][pl.ds(k * sizes[c], sizes[c]), :]

    def whole_band(lists_ref, left_ref, out_ref):
        out_ref[...] = jnp.zeros(out_ref.shape, bf16)
        for g in range(n):
            for s in range(slots):
                for i in range(rb):
                    at = column(lists_ref, i, g * slots + s)
                    add(out_ref, rows_at(at, bs), pl.ds(i * bs, bs), left_ref[g, i, s].T)

    band_shape = shape((BAND * width, width), bf16)
    rows_shapes = [shape((BAND * rb * k, width), bf16) for k in sizes]
    acc_shapes = [shape((WIDE * rb * k, width), f32) for k in sizes]
    own = call(start_rows, [lists, mine], rows_shapes)
    if n == 2:
        (band,) = call(start_band, [lists, *rest], [band_shape])
        rest = [rest[0], *(after(x, band) for x in rest[1:])]
    got = [exchange(x) for x in rest]
    if n == 2:
        left = send(after(mine, got[0]), shift(1), "inner")
    else:
        left = lax.all_gather(p_blocks, "inner", axis=0)
    own = [
        call(end_rows, [lists, own[c], got[c]], [rows_shapes[c]], aliases={1: 0}, us=20 * c)[0]
        for c in chunks
    ]
    if n == 2:
        (band,) = call(end_band, [lists, band, left, *own], [band_shape], aliases={1: 0}, us=20)
    else:
        (band,) = call(whole_band, [lists, left], [band_shape])

    def weights(left_ref, d):
        return left_ref[rows_at(d + REACH, width), :]

    def square_term(d, rows_ref, left_ref, acc_ref):
        term = jnp.dot(rows_ref[...], weights(left_ref, d), preferred_element_type=f32)
        span = rows_ref.shape[0]
        step = span // BAND
        acc_ref[pl.ds(pl.multiple_of((d + REACH) * step, step), span), :] += term

    def square_near(w, u, x, cx, left_ref, acc_ref):
        j = lax.rem(lax.axis_index("rows"), 4)
        d = offsets(j)
        span = w.shape[0]
        edge = span // BAND * REACH
        acc_ref[:edge, :] = jnp.zeros((edge, width), f32)
        acc_ref[edge : edge + span, :] = jnp.dot(
            w[...], left_ref[REACH * width : (REACH + 1) * width, :], preferred_element_type=f32
        )
        acc_ref[edge + span :, :] = jnp.zeros((edge, width), f32)
        square_term(d["core"], u, left_ref, acc_ref)
        square_term(d["x"], x, left_ref, acc_ref)

        @pl.when((j == 1) | (j == 2))
        def _():
            square_term(d["core_x"], cx, left_ref, acc_ref)

    def square_z(acc_in, z, left_ref, acc_ref):
        square_term(offsets(lax.rem(lax.axis_index("rows"), 4))["z"], z, left_ref, acc_ref)

    def square_far(lists_ref, acc_in, cz, left_ref, acc_ref, low_ref):
        j = lax.rem(lax.axis_index("rows"), 4)

        @pl.when((j == 0) | (j == 3))
        def _():
            square_term(offsets(j)["core_z"], cz, left_ref, acc_ref)

        for v in range(fill):
            for i in range(rb):
                where = kept(lists_ref, i, v, low_ref.shape[2])
                low_ref[i, v] = acc_ref[where, pl.ds(i * bs, bs)].astype(bf16)

    def kept(lists_ref, i, v, cols):
        o = lax.axis_index("rows")
        return rows_at(wrapped(lists_ref[v, nb + o * rb + i] - rb * (o - 2 * REACH)), cols)

    def window(d, reach):
        return (WIDE - reach) * rb, jnp.maximum(d, 0) * rb

    def spread(lists_ref, d, reach, low_ref, dense):
        o = lax.axis_index("rows")
        source = lax.rem(o + d + n_rows, n_rows)
        blocks, start = window(d, reach)
        cols = low_ref.shape[2]
        dense[: blocks * cols, :] = jnp.zeros((blocks * cols, width), bf16)
        for v in range(fill):
            for k in range(rb):
                c = wrapped(lists_ref[v, nb + source * rb + k] - rb * (o - 2 * REACH)) - start
                c = jnp.where((c >= 0) & (c < blocks), c, blocks)
                dense[rows_at(c, cols), pl.ds(k * bs, bs)] = low_ref[k, v]

    def multiply(d, reach, dense, left_ref, acc_ref, first=0, end=rb, fresh=False):
        blocks, start = window(d, reach)
        cols = dense.shape[0] // (WIDE * rb + 1)
        rows, lanes = blocks * cols, pl.ds(first * bs, (end - first) * bs)
        term = jnp.dot(
            dense[:rows, :], left_ref[rows_at(d + REACH, width), lanes], preferred_element_type=f32
        )
        if fresh:
            acc_ref[...] = term
        else:
            acc_ref[pl.ds(pl.multiple_of(start * cols, rb * cols), rows), lanes] += term

    def cube_term(lists_ref, d, reach, low_ref, left_ref, dense, acc_ref, first=False):
        spread(lists_ref, d, reach, low_ref, dense)
        multiply(d, reach, dense, left_ref, acc_ref, fresh=first)

    def cube_own(lists_ref, w, u, left_ref, acc_ref, dense):
        d = offsets(lax.rem(lax.axis_index("rows"), 4))
        cube_term(lists_ref, 0, 0, w, left_ref, dense, acc_ref, first=True)
        cube_term(lists_ref, d["core"], 1, u, left_ref, dense, acc_ref)

    def cube_near(lists_ref, acc_in, x, cx, left_ref, acc_ref, dense):
        j = lax.rem(lax.axis_index("rows"), 4)
        d = offsets(j)
        cube_term(lists_ref, d["x"], 2, x, left_ref, dense, acc_ref)

        @pl.when((j == 1) | (j == 2))
        def _():
            cube_term(lists_ref, d["core_x"], 1, cx, left_ref, dense, acc_ref)

    def cube_far(lists_ref, acc_in, z, cz, left_ref, square_ref, acc_ref, keep_ref, give_ref, dense):
        j = lax.rem(lax.axis_index("rows"), 4)
        d = offsets(j)
        cube_term(lists_ref, d["z"], 2, z, left_ref, dense, acc_ref)

        @pl.when((j == 0) | (j == 3))
        def _():
            cube_term(lists_ref, d["core_z"], 1, cz, left_ref, dense, acc_ref)

        results(0, rb, lists_ref, square_ref, acc_ref, keep_ref, give_ref)

    def results(first, end, lists_ref, square_ref, acc_ref, keep_ref, give_ref):
        q = lax.axis_index("inner")

        def result(i, v):
            at = kept(lists_ref, i, v, keep_ref.shape[2]), pl.ds(i * bs, bs)
            return 3.0 * square_ref[at] - 2.0 * acc_ref[at]

        for s in range(slots):
            for i in range(first, end):
                keep_ref[i - first, s] = result(i, q * slots + s)
                for m in range(1, n):
                    v = lax.rem(q + m, n) * slots + s
                    give_ref[m - 1, i - first, s] = result(i, v).astype(bf16)

    def cube_last(lists_ref, acc_in, z, cz, left_ref, square_ref, acc_ref, dense_z, dense_cz, keep_ref, give_ref):
        j = lax.rem(lax.axis_index("rows"), 4)
        d = offsets(j)
        spread(lists_ref, d["z"], 2, z, dense_z)
        multiply(d["z"], 2, dense_z, left_ref, acc_ref, 0, early)

        @pl.when((j == 0) | (j == 3))
        def _():
            spread(lists_ref, d["core_z"], 1, cz, dense_cz)
            multiply(d["core_z"], 1, dense_cz, left_ref, acc_ref, 0, early)

        results(0, early, lists_ref, square_ref, acc_ref, keep_ref, give_ref)

    def cube_end(lists_ref, acc_in, dense_z, dense_cz, left_ref, square_ref, acc_ref, keep_ref, give_ref):
        j = lax.rem(lax.axis_index("rows"), 4)
        d = offsets(j)
        multiply(d["z"], 2, dense_z, left_ref, acc_ref, early)

        @pl.when((j == 0) | (j == 3))
        def _():
            multiply(d["core_z"], 1, dense_cz, left_ref, acc_ref, early)

        results(early, rb, lists_ref, square_ref, acc_ref, keep_ref, give_ref)

    dense = [[pltpu.VMEM(((WIDE * rb + 1) * k, width), bf16)] for k in sizes]
    x, z, sq, low, x2, z2 = [], [], [], [], [], []
    close = []
    for c in chunks:
        u = send(own[c], flip_core)
        x_c = after(send(own[c], flip_x), *own[c + 1 : c + 2], *close)
        z.append(send(x_c, move_z))
        cx = send(x_c, flip_core)
        close += call(square_near, [own[c], u, x_c, cx, band], [acc_shapes[c]], us=20 * c or 20)
        x.append(x_c)
    for c in chunks:
        z_c = after(z[c], close[c])
        cz = after(send(z_c, flip_core), *close[c + 1 : c + 2])
        (acc,) = call(square_z, [close[c], z_c, band], [acc_shapes[c]], aliases={0: 0})
        one = call(
            square_far,
            [lists, acc, cz, band],
            [acc_shapes[c], shape((rb, fill, sizes[c], bs), bf16)],
            aliases={1: 0},
        )
        sq.append(one[0])
        low.append(one[1])
    keep, give, near = [], [], []
    for c in chunks:
        x_c = send(low[c], flip_x)
        u = send(low[c], flip_core)
        (acc,) = call(
            cube_own, [lists, low[c], u, after(band, low[-1], *near)], [acc_shapes[c]], dense[c], us=20 * c
        )
        x2.append(x_c)
        z2.append(send(x_c, move_z))
        cx = send(x_c, flip_core)
        (acc,) = call(cube_near, [lists, acc, x_c, cx, band], [acc_shapes[c]], dense[c], aliases={1: 0}, us=20 * c)
        near.append(acc)
    early = rb - rb // 3

    def result_shapes(c, count):
        kept_shape = (count, slots, sizes[c], bs)
        return [shape(kept_shape, f32), shape((n - 1, *kept_shape), bf16)]

    taken = []
    for c in chunks[:-1]:
        z_c = after(z2[c], near[c], *give)
        one = call(
            cube_far,
            [lists, near[c], z_c, send(z_c, flip_core), band, sq[c]],
            [acc_shapes[c], *result_shapes(c, rb)],
            dense[c],
            aliases={1: 0},
        )[1:]
        keep.append(one[0])
        give.append(one[1])
        taken.append(exchange(one[1]))
    c = cuts - 1
    z_c = after(z2[c], near[c], *give)
    dense_shape = shape(dense[c][0].shape, bf16)
    acc, dense_z, dense_cz, keep_a, give_a = call(
        cube_last,
        [lists, near[c], z_c, send(z_c, flip_core), band, sq[c]],
        [acc_shapes[c], dense_shape, dense_shape, *result_shapes(c, early)],
        aliases={1: 0},
    )
    taken_a = exchange(give_a)
    _, keep_b, give_b = call(
        cube_end,
        [lists, acc, dense_z, dense_cz, band, sq[c]],
        [acc_shapes[c], *result_shapes(c, rb - early)],
        aliases={1: 0},
    )
    taken_b = exchange(give_b)

    def join(first, end, keep_refs, taken_refs, out_ref, turned, done, sems):
        q = lax.axis_index("inner")
        copies = {i: pltpu.make_async_copy(done.at[i], out_ref.at[i], sems.at[i]) for i in range(first, end)}
        for i in range(first, end):
            for s in range(slots):
                for c in chunks:
                    k = i - first if c == cuts - 1 else i
                    turned[i, s, piece(q, c), :] = keep_refs[c][k, s]
                    for m in range(1, n):
                        at = piece(lax.rem(q - m + n, n), c)
                        turned[i, s, at, :] = taken_refs[c][m - 1, k, s].astype(f32)
                done[i, s] = turned[i, s].T
            copies[i].start()
        for copy in copies.values():
            copy.wait()

    def join_first(*refs):
        join(0, early, refs[:cuts], refs[cuts : 2 * cuts], *refs[2 * cuts :])

    def join_rest(*refs):
        join(early, rb, refs[:cuts], refs[cuts : 2 * cuts], *refs[2 * cuts + 1 :])

    whole = pltpu.VMEM((rb, slots, bs, bs), f32)
    scratch = [whole, whole, pltpu.SemaphoreType.DMA((rb,))]
    out_shape = [shape((rb, slots, bs, bs), f32)]
    (out,) = call(join_first, [*keep, keep_a, *taken, taken_a], out_shape, scratch, hbm_out=True)
    (out,) = call(
        join_rest,
        [*keep, keep_b, *taken, taken_b, out],
        out_shape,
        scratch,
        aliases={2 * cuts: 0},
        hbm_in=(2 * cuts,),
        hbm_out=True,
    )
    return out


def solution(mesh):
    in_specs = (P("rows", "inner", None, None), P(), P())
    out_specs = P("rows", "inner", None, None)
    return jax.shard_map(
        per_device, mesh=mesh, in_specs=in_specs, out_specs=out_specs, check_vma=False
    )
```
